512 devices in a mesh: leaf: 16 (over y, core), blk: 32 (over z, x).
Axes of the slice: x: 4, y: 8, z: 8, core: 2. Of those that a mesh axis runs over, the one named last changes fastest.
Arguments:
- adjoint_rhs: float32 [128, 128, 64], P('leaf'), may hold values from -6 to 6
- diag_inverse: float32 [128, 128, 128], P('leaf'), may hold values from -1 to 2
- blocks: float32 [16, 32, 32, 128, 128], P('leaf', 'blk'), may hold values from -0.03125 to 0.03125
- block_rows: int32 [16, 32, 32], P('leaf', 'blk'), may hold values from 0 to 127, as said below
- block_cols: int32 [16, 32, 32], P('leaf', 'blk'), may hold values from 0 to 7
- block_count: int32 [16, 32], P('leaf', 'blk'), may hold values from 0 to 32, as said below
- node_level: int32 [16], replicated, may hold values from 0 to 3, as said below
Outputs:
- adjoint_solution: float32 [128, 128, 64], P('leaf')
The draws below stay inside these ranges and needn't reach their ends.
Inputs may be any that keep to these rules, and one draw needn't show every extreme that they name: `node_level`: exactly one node has level 0, and every level up to 3 is held by some node. `block_rows`: every live slot names a block row of a node whose level is lower than that of the slot's own node. `block_count`: the node of level 0 has no live slots; every other node has one device with exactly 32 live slots.
All inputs are finite; a program needn't handle non-finite values.
Results may differ from the reference program's by a relative error of at most 0.0003.
Values sent between devices are 32-bit elements; how exact they have to be, the bound alone decides.
A program may use at most 64 MiB of HBM per device.

```python
import math
import jax
import jax.numpy as jnp
from jax import lax

BS = 128
NBC = 8
LEVELS = 4
BPD = 32
NRHS = 64
NCOLS = 128
N_LEAF = 16
N_BLK = 32


def tree_draw(key):
    base_key = jax.random.fold_in(key, 101)
    key_order, key_depth, key_parent = jax.random.split(base_key, 3)
    shuffle = jax.random.permutation(key_order, N_LEAF)
    deeper = jax.random.randint(key_depth, (N_LEAF,), 1, LEVELS)
    position = jnp.arange(N_LEAF, dtype=jnp.int32)
    by_position = jnp.where(position < LEVELS, position, deeper).astype(jnp.int32)
    depth_of = jnp.zeros((N_LEAF,), jnp.int32).at[shuffle].set(by_position)
    scores = jax.random.randint(key_parent, (N_LEAF, N_LEAF), 0, 1000) * N_LEAF + position[None, :]
    allowed = depth_of[None, :] == depth_of[:, None] - 1
    parent = jnp.argmax(jnp.where(allowed, scores, -1), axis=1).astype(jnp.int32)
    return (depth_of, parent)


def slot_draw(key):
    depth_of, parent = tree_draw(key)
    key_climb, key_row, key_col, key_count, key_busy = jax.random.split(jax.random.fold_in(key, 202), 5)
    slot_shape = (N_LEAF, N_BLK, BPD)
    climbs = jax.random.randint(key_climb, slot_shape, 0, 1 << 20) % jnp.maximum(depth_of, 1)[:, None, None] + 1
    ancestor = jnp.broadcast_to(jnp.arange(N_LEAF, dtype=jnp.int32)[:, None, None], slot_shape)
    for section in range(LEVELS - 1):
        ancestor = jnp.where(section < climbs, parent[ancestor], ancestor)
    row_ids = ancestor * NBC + jax.random.randint(key_row, slot_shape, 0, NBC)
    col_ids = jax.random.randint(key_col, slot_shape, 0, NBC)
    counts = jax.random.randint(key_count, (N_LEAF, N_BLK), BPD // 8, BPD + 1)
    busiest = jax.random.randint(key_busy, (N_LEAF,), 0, N_BLK)
    counts = jnp.where(jnp.arange(N_BLK)[None, :] == busiest[:, None], BPD, counts)
    counts = jnp.where(depth_of[:, None] == 0, 0, counts)
    return (row_ids.astype(jnp.int32), col_ids.astype(jnp.int32), counts.astype(jnp.int32))


def draw_node_level(key, part):
    return tree_draw(key)[0]


def draw_block_rows(key, part):
    return slot_draw(key)[0]


def draw_block_cols(key, part):
    return slot_draw(key)[1]


def draw_block_count(key, part):
    return slot_draw(key)[2]


def draw_diag_inverse(key, part):
    noise_key = jax.random.fold_in(key, 303)
    noise = jnp.clip(jax.random.normal(noise_key, (NCOLS, BS, BS), jnp.float32), -4.0, 4.0)
    return jnp.eye(BS, dtype=jnp.float32)[None] + noise * (0.3 / math.sqrt(BS))


def block_levels(stream_key, shape, pieces, least, top_value):
    level = 1.0
    for axis_at, blocks in pieces:
        steps = jax.random.uniform(jax.random.fold_in(jax.random.fold_in(stream_key, 6), axis_at), (blocks,), jnp.float32, least / len(pieces), top_value / len(pieces))
        level = level * jnp.repeat(jnp.exp(steps), shape[axis_at] // blocks).reshape((-1,) + (1,) * (len(shape) - 1 - axis_at))
    return level


def normal_values(stream_key, extent, scale, bound, cuts=(), kind=jnp.bfloat16):
    drawn = scale * jax.random.normal(stream_key, extent, jnp.float32)
    if cuts:
        drawn = drawn * block_levels(stream_key, extent, cuts, -0.22, 0.18)
    return jnp.clip(drawn, -bound, bound).astype(kind)


def setup_inputs(seed: int = 0) -> dict:
    arg_keys = jax.random.split(jax.random.key(seed), 8)
    adjoint_rhs = normal_values(arg_keys[0], (NCOLS, BS, NRHS), 1.0, 6.0, ((0, 16),), jnp.float32)
    diag_inverse = draw_diag_inverse(jax.random.fold_in(arg_keys[7], 71), 0)
    blocks = normal_values(arg_keys[2], (N_LEAF, N_BLK, BPD, BS, BS), (2 * BS * N_BLK * BPD // NBC) ** -0.5, 0.03125, ((0, 16), (1, 32)), jnp.float32)
    block_rows = draw_block_rows(jax.random.fold_in(arg_keys[7], 71), 0)
    block_cols = draw_block_cols(jax.random.fold_in(arg_keys[7], 71), 0)
    block_count = draw_block_count(jax.random.fold_in(arg_keys[7], 71), 0)
    node_level = draw_node_level(jax.random.fold_in(arg_keys[7], 71), 0)
    return dict(adjoint_rhs=adjoint_rhs, diag_inverse=diag_inverse, blocks=blocks, block_rows=block_rows, block_cols=block_cols, block_count=block_count, node_level=node_level)


def reference(adjoint_rhs, diag_inverse, blocks, block_rows, block_cols, block_count, node_level):
    nodes_total = node_level.shape[0]
    per_node = adjoint_rhs.shape[0] // nodes_total
    width = adjoint_rhs.shape[1]
    columns = adjoint_rhs.shape[2]
    sequence = jnp.argsort(node_level, stable=True).astype(jnp.int32)

    def node_step(solved, member):
        def device_loop(peer_at, partial_value):
            def slot_loop(slot_at, inner):
                tile = blocks[member, peer_at, slot_at]
                row_at = block_rows[member, peer_at, slot_at]
                col_at = block_cols[member, peer_at, slot_at]
                panel_row = lax.dynamic_index_in_dim(solved, row_at, 0, keepdims=False)
                product = lax.dot_general(tile, panel_row, (((0,), (0,)), ((), ())), precision=lax.Precision.HIGHEST)
                current = lax.dynamic_index_in_dim(inner, col_at, 0, keepdims=False)
                return lax.dynamic_update_index_in_dim(inner, current + product, col_at, 0)
            return lax.fori_loop(0, block_count[member, peer_at], slot_loop, partial_value)
        summed = lax.fori_loop(0, N_BLK, device_loop, jnp.zeros((per_node, width, columns), jnp.float32))
        offset = (member * per_node).astype(jnp.int32)
        own_rhs = lax.dynamic_slice_in_dim(adjoint_rhs, offset, per_node, 0)
        own_inverse = lax.dynamic_slice_in_dim(diag_inverse, offset, per_node, 0)
        updated = jnp.einsum("cij,cjk->cik", own_inverse, own_rhs - summed, precision=lax.Precision.HIGHEST)
        return lax.dynamic_update_slice_in_dim(solved, updated, offset, 0), None

    solved, _ = lax.scan(node_step, jnp.zeros_like(adjoint_rhs), sequence)
    return solved
```

```python
import functools

import jax
import jax.numpy as jnp
from jax import lax
from jax.experimental import pallas as pl
from jax.experimental.pallas import tpu as pltpu
from jax.sharding import PartitionSpec as P

LEVELS = 4
MESH = pl.DeviceIdType.MESH
F32 = jnp.float32
BF16 = jnp.bfloat16


def split(value):
    high = value.astype(BF16)
    return high, (value - high.astype(F32)).astype(BF16)


def kernel(
    cap, nl, nz, nx, slots, quarter, width,
    level_ref, rows_ref, cols_ref, count_ref, rhs_hbm, dinv_hbm, tiles_hbm,
    out_ref,
    tiles, dinv, rhs, rhs_t, weights, prods, part, from_x, to_z, from_z, piece, leaf0, leaf1, leaf2, gather0, gather1, gather2,
    final, mine, rank, names, slot_node, slot_level,
    local_sems, leaf_send, leaf_recv, rsx_send, rsx_recv, rsz_send, rsz_recv, agz_send, agz_recv, agx_send, agx_recv,
    core_send, core_recv,
):
    half = quarter // 2
    leaf, blk = lax.axis_index("leaf"), lax.axis_index("blk")
    core = lax.rem(leaf, 2)
    z, x = lax.div(blk, nx), lax.rem(blk, nx)
    gathers = (gather0, gather1, gather2)
    from_leaf = (leaf0, leaf1, leaf2)

    def z_peer(k):
        return lax.rem(z + k, nz)

    def x_peer(k):
        return lax.rem(x + k, nx)

    def at_z(k):
        return (leaf, z_peer(k) * nx + x)

    def at_x(k):
        return (leaf, z * nx + x_peer(k))

    def at_leaf(k):
        return (lax.rem(leaf + k, nl), blk)

    sibling = (leaf + 1 - 2 * core, blk)

    copies = [
        pltpu.make_async_copy(dinv_hbm.at[z], dinv, local_sems.at[0]),
        pltpu.make_async_copy(rhs_hbm.at[z], rhs, local_sems.at[1]),
        pltpu.make_async_copy(tiles_hbm, tiles, local_sems.at[2]),
    ]
    for copy in copies:
        copy.start()

    barrier = pltpu.get_barrier_semaphore()
    partners = [at_leaf(k) for k in range(1, nl)] + [at_z(k) for k in range(1, nz)] + [at_x(k) for k in range(1, nx)]
    for partner in partners:
        pl.semaphore_signal(barrier, inc=1, device_id=partner, device_id_type=MESH)

    for node in range(nl):
        at = jnp.int32(0)
        for other in range(node):
            at = at + jnp.where(level_ref[other] == level_ref[node], 1, 0)
        rank[node] = at
    for level in range(LEVELS - 1):
        for j in range(1 if level == 0 else cap):
            name = jnp.int32(0)
            for node in range(nl):
                name = name + jnp.where((level_ref[node] == level) & (rank[node] == j), node, 0)
            names[level * cap + j] = name

    def read_slot(s, _):
        node = lax.div(rows_ref[0, 0, s], nz)
        slot_node[s] = jnp.minimum(rank[node], cap - 1)
        slot_level[s] = jnp.where(s < count_ref[0, 0], level_ref[node], -1)
        return 0

    lax.fori_loop(0, slots, read_slot, 0)
    my_level = level_ref[leaf]

    copies[0].wait()
    copies[1].wait()
    rhs_t[...] = rhs[...].T
    own_rhs = rhs_t[pl.ds(pl.multiple_of(x * quarter, 8), quarter), :]

    def solve(summed):
        return lax.dot_general(
            own_rhs - summed, dinv[...], (((1,), (1,)), ((), ())),
            precision=lax.Precision.HIGHEST, preferred_element_type=F32,
        )

    piece[0] = solve(jnp.zeros((quarter, width), F32))
    mine[...] = piece[0]
    pl.semaphore_wait(barrier, len(partners))

    def wait_recv(ref, sem):
        pltpu.make_async_copy(ref, ref, sem).wait()

    def send(src, dst, send_sem, recv_sem, device):
        pltpu.make_async_remote_copy(
            src_ref=src, dst_ref=dst, send_sem=send_sem, recv_sem=recv_sem, device_id=device, device_id_type=MESH
        ).start()

    def leaf_start(level):
        for k in range(1, nl):
            peer = at_leaf(k)
            rows = pl.ds(pl.multiple_of(lax.rem(peer[0], 2) * half, 8), half)
            send(piece.at[level, rows], from_leaf[level].at[leaf], leaf_send.at[level], leaf_recv.at[level], peer)
        from_leaf[level][leaf] = piece[level, pl.ds(pl.multiple_of(core * half, 8), half), :]

    def broadcast(level):
        box = gathers[level]
        wait_recv(from_leaf[level].at[pl.ds(0, nl - 1)], leaf_recv.at[level])
        for j in range(1 if level == 0 else cap):
            box[core, x, z, j] = from_leaf[level][names[level * cap + j]]
        own = box.at[core, x, z]
        for k in range(1, nz):
            send(own, own, agz_send.at[level], agz_recv.at[level], at_z(k))
        wait_recv(box.at[core, x, pl.ds(0, nz - 1)], agz_recv.at[level])
        line = box.at[core, x]
        for k in range(1, nx):
            send(line, line, agx_send.at[level], agx_recv.at[level, k - 1], at_x(k))
        send(line, line, core_send.at[level], core_recv.at[level], sibling)
        for k in range(1, nx):
            wait_recv(line, agx_recv.at[level, k - 1])
            got = box.at[core, lax.rem(x + nx - k, nx)]
            send(got, got, core_send.at[level], core_recv.at[level], sibling)
        wait_recv(box.at[core], core_recv.at[level])

    def products(level):
        box = gathers[level - 1]

        def one(s, _):
            node = slot_node[s] if level > 1 else 0
            at = lax.rem(rows_ref[0, 0, s], nz)
            panel = jnp.concatenate([box[h, q, at, node] for q in range(nx) for h in range(2)], axis=0)
            high, low = split(panel)
            both = jnp.concatenate([high, low], axis=0)
            got = jnp.dot(both, weights[s], preferred_element_type=F32)
            n = nx * quarter
            prods[s] = (got[:n, width:] + got[n:, :width]) + got[:n, :width]
            return 0

        lax.fori_loop(0, slots, one, 0, unroll=4)

        def column(c, _):
            total = jnp.zeros((nx * quarter, width), F32)
            for s in range(slots):
                key = jnp.where(slot_level[s] == level - 1, cols_ref[0, 0, s], -1)
                total = total + jnp.where(key == c, 1.0, 0.0).astype(F32) * prods[s]
            for q in range(nx):
                mass = total[q * quarter : (q + 1) * quarter]
                part[q, c] = mass if level == 1 else part[q, c] + mass
            return 0

        lax.fori_loop(0, nz, column, 0)

    def reduce(level):
        at = level - 1
        for k in range(1, nx):
            send(part.at[x_peer(k)], from_x.at[at, k - 1], rsx_send.at[at], rsx_recv.at[at], at_x(k))
        wait_recv(from_x.at[at], rsx_recv.at[at])
        total = part[x]
        for k in range(nx - 1):
            total = total + from_x[at, k]
        to_z[at] = total
        for k in range(1, nz):
            send(to_z.at[at, z_peer(k)], from_z.at[at, k - 1], rsz_send.at[at], rsz_recv.at[at], at_z(k))
        wait_recv(from_z.at[at], rsz_recv.at[at])
        total = to_z[at, z]
        for k in range(nz - 1):
            total = total + from_z[at, k]
        return total

    def drain_part(level):
        wait_recv(from_x.at[level - 1], rsx_send.at[level - 1])

    leaf_start(0)
    copies[2].wait()

    def prepare(s, _):
        high, low = split(tiles[s])
        weights[s, :, :width] = high
        weights[s, :, width:] = low
        return 0

    lax.fori_loop(0, slots, prepare, 0, unroll=2)
    broadcast(0)
    for level in range(1, LEVELS):
        if level > 1:
            drain_part(level - 1)
        products(level)
        solved = solve(reduce(level))
        piece[level] = solved
        keep = jnp.where(my_level == level, 1.0, 0.0).astype(F32)
        mine[...] = keep * solved + (1.0 - keep) * mine[...]
        if level + 1 < LEVELS:
            leaf_start(level)
            broadcast(level)

    last = LEVELS - 1
    final[x, z] = mine[...]
    own = final.at[x, z]
    for k in range(1, nz):
        send(own, own, agz_send.at[last], agz_recv.at[last], at_z(k))
    wait_recv(final.at[x, pl.ds(0, nz - 1)], agz_recv.at[last])
    line = final.at[x]
    for k in range(1, nx):
        send(line, line, agx_send.at[last], agx_recv.at[last, k - 1], at_x(k))
    for k in range(1, nx):
        wait_recv(line, agx_recv.at[last, k - 1])
    for q in range(nx):
        out_ref[:, pl.ds(q * quarter, quarter), :] = final[q]

    drain_part(last)
    for at in range(LEVELS - 1):
        wait_recv(from_z.at[at], rsz_send.at[at])
        wait_recv(from_leaf[at].at[pl.ds(0, nl - 1)], leaf_send.at[at])
        box = gathers[at]
        wait_recv(box.at[0, 0, pl.ds(0, nz - 1)], agz_send.at[at])
        wait_recv(box.at[0, pl.ds(0, nx - 1)], agx_send.at[at])
        wait_recv(box.at[0], core_send.at[at])
    wait_recv(final.at[0, pl.ds(0, nz - 1)], agz_send.at[last])
    wait_recv(final.at[pl.ds(0, nx - 1)], agx_send.at[last])


def body(cap, adjoint_rhs, diag_inverse, blocks, block_rows, block_cols, block_count, node_level):
    per_node, width, columns = adjoint_rhs.shape
    slots = blocks.shape[2]
    nl, nb = lax.axis_size("leaf"), lax.axis_size("blk")
    nz = per_node
    nx = nb // nz
    quarter = columns // nx
    half = quarter // 2
    last = LEVELS - 1
    dma = pltpu.SemaphoreType.DMA
    smem = pl.BlockSpec(memory_space=pltpu.SMEM)
    hbm = pl.BlockSpec(memory_space=pl.ANY)
    vmem = pltpu.VMEM
    solved = pl.pallas_call(
        functools.partial(kernel, cap, nl, nz, nx, slots, quarter, width),
        out_shape=jax.ShapeDtypeStruct((per_node, columns, width), F32),
        in_specs=[smem] * 4 + [hbm] * 3,
        out_specs=pl.BlockSpec(memory_space=pltpu.VMEM),
        scratch_shapes=[
            vmem((slots, width, width), F32),
            vmem((width, width), F32),
            vmem((width, columns), F32),
            vmem((columns, width), F32),
            vmem((slots, width, 2 * width), BF16),
            vmem((slots, columns, width), F32),
            vmem((nx, nz, quarter, width), F32),
            vmem((last, nx - 1, nz, quarter, width), F32),
            vmem((last, nz, quarter, width), F32),
            vmem((last, nz - 1, quarter, width), F32),
            vmem((LEVELS, quarter, width), F32),
            vmem((nl, half, width), F32),
            vmem((nl, half, width), F32),
            vmem((nl, half, width), F32),
            vmem((2, nx, nz, 1, half, width), F32),
            vmem((2, nx, nz, cap, half, width), F32),
            vmem((2, nx, nz, cap, half, width), F32),
            vmem((nx, nz, quarter, width), F32),
            vmem((quarter, width), F32),
            pltpu.SMEM((nl,), jnp.int32),
            pltpu.SMEM((last * cap,), jnp.int32),
            pltpu.SMEM((slots,), jnp.int32),
            pltpu.SMEM((slots,), jnp.int32),
            dma((3,)),
            dma((last,)),
            dma((last,)),
            dma((last,)),
            dma((last,)),
            dma((last,)),
            dma((last,)),
            dma((LEVELS,)),
            dma((LEVELS,)),
            dma((LEVELS,)),
            dma((LEVELS, nx - 1)),
            dma((last,)),
            dma((last,)),
        ],
        compiler_params=pltpu.CompilerParams(
            collective_id=0, has_side_effects=True, vmem_limit_bytes=48 * 1024 * 1024
        ),
        name="tree_solve",
    )(
        node_level, block_rows.reshape(1, 1, slots), block_cols.reshape(1, 1, slots), block_count,
        adjoint_rhs, diag_inverse, blocks.reshape(slots, width, width),
    )
    return jnp.swapaxes(solved, 1, 2)


def solution(mesh):
    in_specs = (
        P("leaf", None, None),
        P("leaf", None, None),
        P("leaf", "blk", None, None, None),
        P("leaf", "blk", None),
        P("leaf", "blk", None),
        P("leaf", "blk"),
        P(),
    )
    out_specs = P("leaf", None, None)
    cap = mesh.shape["leaf"] - 3
    return jax.shard_map(
        functools.partial(body, cap), mesh=mesh, in_specs=in_specs, out_specs=out_specs, check_vma=False
    )
```

```python
import functools

import jax
import jax.numpy as jnp
from jax import lax
from jax.experimental import pallas as pl
from jax.experimental.pallas import tpu as pltpu
from jax.sharding import PartitionSpec as P

LEVELS = 4
VMEM_LIMIT = 60 * 1024 * 1024
MESH = pl.DeviceIdType.MESH
F32 = jnp.float32
BF16 = jnp.bfloat16


def split(value):
    high = value.astype(BF16)
    return high, (value - high.astype(F32)).astype(BF16)


def kernel(
    cap, nl, nz, nx, slots, quarter, width,
    level_hbm, rows_hbm, cols_hbm, count_hbm, rhs_hbm, dinv_hbm, tiles_hbm,
    out_ref, flag_ref,
    level_ref, rows_ref, cols_ref, count_ref,
    tiles, dinv, own_rhs, weights, prods, part, from_x, to_z, from_z, piece, leaf0, leaf1, leaf2, gather0, gather1, gather2,
    final, mine, need, need_z, need_x, flags, rank, names, slot_node, slot_level,
    local_sems, leaf_send, leaf_recv, rsx_send, rsx_recv, rsz_send, rsz_recv, agz_send, agz_recv, agx_send, agx_recv,
    core_send, core_recv, need_send, need_recv,
):
    fast = cap == 0
    half = quarter // 2
    leaf, blk = lax.axis_index("leaf"), lax.axis_index("blk")
    core = lax.rem(leaf, 2)
    z, x = lax.div(blk, nx), lax.rem(blk, nx)
    gathers = (gather0, gather1, gather2)
    from_leaf = (leaf0, leaf1, leaf2)

    def z_peer(k):
        return lax.rem(z + k, nz)

    def x_peer(k):
        return lax.rem(x + k, nx)

    def at_z(k):
        return (leaf, z_peer(k) * nx + x)

    def at_x(k):
        return (leaf, z * nx + x_peer(k))

    def at_leaf(k):
        return (lax.rem(leaf + k, nl), blk)

    sibling = (leaf + 1 - 2 * core, blk)

    barrier = pltpu.get_barrier_semaphore()
    partners = [at_leaf(k) for k in range(1, nl)] + [at_z(k) for k in range(1, nz)] + [at_x(k) for k in range(1, nx)]
    for partner in partners:
        pl.semaphore_signal(barrier, inc=1, device_id=partner, device_id_type=MESH)

    copies = [
        pltpu.make_async_copy(dinv_hbm.at[z], dinv, local_sems.at[0]),
        pltpu.make_async_copy(
            rhs_hbm.at[z, pl.ds(pl.multiple_of(x * quarter, 8), quarter)], own_rhs, local_sems.at[1]
        ),
        pltpu.make_async_copy(level_hbm, level_ref, local_sems.at[2]),
        pltpu.make_async_copy(rows_hbm, rows_ref, local_sems.at[3]),
        pltpu.make_async_copy(cols_hbm, cols_ref, local_sems.at[4]),
        pltpu.make_async_copy(count_hbm, count_ref, local_sems.at[5]),
        pltpu.make_async_copy(tiles_hbm, tiles, local_sems.at[6]),
    ]
    for copy in copies:
        copy.start()

    def solve(summed):
        return lax.dot_general(
            own_rhs[...] - summed, dinv[...], (((1,), (1,)), ((), ())),
            precision=lax.Precision.HIGHEST, preferred_element_type=F32,
        )

    copies[0].wait()
    copies[1].wait()
    piece[0] = solve(jnp.zeros((quarter, width), F32))
    mine[...] = piece[0]
    for copy in copies[2:6]:
        copy.wait()

    if fast:
        root = jnp.int32(0)
        for node in range(nl):
            root = jnp.maximum(root, jnp.where(level_ref[node] == 0, node, 0))
        names[0] = root
    else:
        for node in range(nl):
            at = jnp.int32(0)
            for other in range(node):
                at = at + jnp.where(level_ref[other] == level_ref[node], 1, 0)
            rank[node] = at
        for level in range(LEVELS - 1):
            for j in range(1 if level == 0 else cap):
                name = jnp.int32(0)
                for node in range(nl):
                    name = name + jnp.where((level_ref[node] == level) & (rank[node] == j), node, 0)
                names[level * cap + j] = name

    def read_slot(s, seen):
        node = lax.div(rows_ref[0, 0, s], nz)
        level = jnp.where(s < count_ref[0, 0], level_ref[node], -1)
        slot_level[s] = level
        if not fast:
            slot_node[s] = jnp.minimum(rank[node], cap - 1)
        top1, low1, top2, low2 = seen
        return (
            jnp.maximum(top1, jnp.where(level == 1, node, -1)),
            jnp.maximum(low1, jnp.where(level == 1, -node, -nl)),
            jnp.maximum(top2, jnp.where(level == 2, node, -1)),
            jnp.maximum(low2, jnp.where(level == 2, -node, -nl)),
        )

    first = (jnp.int32(-1), jnp.int32(-nl), jnp.int32(-1), jnp.int32(-nl))
    seen = lax.fori_loop(0, slots, read_slot, first)
    my_level = level_ref[leaf]
    pl.semaphore_wait(barrier, len(partners))

    def wait_bytes(ref, sem):
        pltpu.make_async_copy(ref, ref, sem).wait()

    drains = []

    def send(src, dst, send_sem, recv_sem, device):
        pltpu.make_async_remote_copy(
            src_ref=src, dst_ref=dst, send_sem=send_sem, recv_sem=recv_sem, device_id=device, device_id_type=MESH
        ).start()

    def halves(level):
        return level == 0 or not fast

    def leaf_start(level):
        for k in range(1, nl):
            peer = at_leaf(k)
            rows = pl.ds(pl.multiple_of(lax.rem(peer[0], 2) * half, 8), half)
            src = piece.at[level, rows] if halves(level) else piece.at[level]
            send(src, from_leaf[level].at[leaf], leaf_send.at[level], leaf_recv.at[level], peer)
        if halves(level):
            from_leaf[level][leaf] = piece[level, pl.ds(pl.multiple_of(core * half, 8), half), :]
        else:
            from_leaf[level][leaf] = piece[level]
        drains.append((from_leaf[level].at[pl.ds(0, nl - 1)], leaf_send.at[level]))

    def broadcast_listed(level):
        box = gathers[level]
        wait_bytes(from_leaf[level].at[pl.ds(0, nl - 1)], leaf_recv.at[level])
        for j in range(1 if level == 0 else cap):
            box[core, x, z, j] = from_leaf[level][names[level * cap + j]]
        own = box.at[core, x, z]
        for k in range(1, nz):
            send(own, own, agz_send.at[level], agz_recv.at[level], at_z(k))
        if level == 0 and fast:
            need_across()
        wait_bytes(box.at[core, x, pl.ds(0, nz - 1)], agz_recv.at[level])
        line = box.at[core, x]
        for k in range(1, nx):
            send(line, line, agx_send.at[level], agx_recv.at[level, k - 1], at_x(k))
        send(line, line, core_send.at[level], core_recv.at[level], sibling)
        for k in range(1, nx):
            wait_bytes(line, agx_recv.at[level, k - 1])
            got = box.at[core, lax.rem(x + nx - k, nx)]
            send(got, got, core_send.at[level], core_recv.at[level], sibling)
        wait_bytes(box.at[core], core_recv.at[level])
        drains.append((box.at[0, 0, pl.ds(0, nz - 1)], agz_send.at[level]))
        drains.append((box.at[0, pl.ds(0, nx - 1)], agx_send.at[level]))
        drains.append((box.at[0], core_send.at[level]))

    def gather_plane(box, value, level):
        box[x, z] = value
        own = box.at[x, z]
        for k in range(1, nz):
            send(own, own, agz_send.at[level], agz_recv.at[level], at_z(k))
        wait_bytes(box.at[x, pl.ds(0, nz - 1)], agz_recv.at[level])
        line = box.at[x]
        for k in range(1, nx):
            send(line, line, agx_send.at[level], agx_recv.at[level, 0], at_x(k))
        wait_bytes(box.at[pl.ds(0, nx - 1)], agx_recv.at[level, 0])
        drains.append((box.at[0, pl.ds(0, nz - 1)], agz_send.at[level]))
        drains.append((box.at[pl.ds(0, nx - 1)], agx_send.at[level]))

    def broadcast(level):
        if halves(level):
            broadcast_listed(level)
            return
        wait_bytes(from_leaf[level].at[pl.ds(0, nl - 1)], leaf_recv.at[level])
        wanted = need[2 * level - 2 : 2 * level - 1, :]
        chosen = jnp.zeros((quarter, width), F32)
        for node in range(nl):
            chosen = jnp.where(wanted == float(node), from_leaf[level][node], chosen)
        gather_plane(gathers[level], chosen, level)

    def need_start():
        at = lax.broadcasted_iota(jnp.int32, (8, width), 0)
        tile = jnp.full((8, width), -float(nl), F32)
        for i, value in enumerate(seen):
            tile = jnp.where(at == i, value.astype(F32), tile)
        need[...] = tile
        for k in range(1, nz):
            send(need, need_z.at[k - 1], need_send.at[0], need_recv.at[0], at_z(k))

    def need_across():
        wait_bytes(need_z, need_recv.at[0])
        wait_bytes(need_z, need_send.at[0])
        tile = need[...]
        for k in range(nz - 1):
            tile = jnp.maximum(tile, need_z[k])
        need[...] = tile
        for k in range(1, nx):
            send(need, need_x.at[k - 1], need_send.at[1], need_recv.at[1], at_x(k))

    def need_end():
        wait_bytes(need_x, need_recv.at[1])
        wait_bytes(need_x, need_send.at[1])
        tile = need[...]
        for k in range(nx - 1):
            tile = jnp.maximum(tile, need_x[k])
        need[...] = tile
        several = (tile[0:1] + tile[1:2] > 0.0) | (tile[2:3] + tile[3:4] > 0.0)
        flags[leaf] = jnp.where(jnp.broadcast_to(several, (8, width)), 1.0, 0.0).astype(F32)
        for k in range(1, nl):
            send(flags.at[leaf], flags.at[leaf], need_send.at[2], need_recv.at[2], at_leaf(k))
        drains.append((flags.at[pl.ds(0, nl - 1)], need_send.at[2]))

    def products(level):
        box = gathers[level - 1]

        def one(s, _):
            at = lax.rem(rows_ref[0, 0, s], nz)
            if halves(level - 1):
                node = slot_node[s] if level > 1 else 0
                panel = jnp.concatenate([box[h, q, at, node] for q in range(nx) for h in range(2)], axis=0)
            else:
                panel = jnp.concatenate([box[q, at] for q in range(nx)], axis=0)
            high, low = split(panel)
            both = jnp.concatenate([high, low], axis=0)
            got = jnp.dot(both, weights[s], preferred_element_type=F32)
            n = nx * quarter
            prods[s] = (got[:n, width:] + got[n:, :width]) + got[:n, :width]
            return 0

        lax.fori_loop(0, slots, one, 0, unroll=4)

        def column(c, _):
            total = jnp.zeros((nx * quarter, width), F32)
            for s in range(slots):
                key = jnp.where(slot_level[s] == level - 1, cols_ref[0, 0, s], -1)
                total = total + jnp.where(key == c, 1.0, 0.0).astype(F32) * prods[s]
            for q in range(nx):
                mass = total[q * quarter : (q + 1) * quarter]
                part[q, c] = mass if level == 1 else part[q, c] + mass
            return 0

        lax.fori_loop(0, nz, column, 0)

    def reduce(level):
        at = level - 1
        for k in range(1, nx):
            send(part.at[x_peer(k)], from_x.at[at, k - 1], rsx_send.at[at], rsx_recv.at[at], at_x(k))
        if level == 1 and fast:
            need_end()
        wait_bytes(from_x.at[at], rsx_recv.at[at])
        total = part[x]
        for k in range(nx - 1):
            total = total + from_x[at, k]
        to_z[at] = total
        for k in range(1, nz):
            send(to_z.at[at, z_peer(k)], from_z.at[at, k - 1], rsz_send.at[at], rsz_recv.at[at], at_z(k))
        wait_bytes(from_z.at[at], rsz_recv.at[at])
        total = to_z[at, z]
        for k in range(nz - 1):
            total = total + from_z[at, k]
        drains.append((from_z.at[at], rsz_send.at[at]))
        return total

    def drain_part(level):
        wait_bytes(from_x.at[level - 1], rsx_send.at[level - 1])

    leaf_start(0)
    if fast:
        need_start()
    copies[6].wait()

    def prepare(s, _):
        high, low = split(tiles[s])
        weights[s, :, :width] = high
        weights[s, :, width:] = low
        return 0

    lax.fori_loop(0, slots, prepare, 0, unroll=2)
    broadcast(0)
    for level in range(1, LEVELS):
        if level > 1:
            drain_part(level - 1)
        products(level)
        solved = solve(reduce(level))
        piece[level] = solved
        keep = jnp.where(my_level == level, 1.0, 0.0).astype(F32)
        mine[...] = keep * solved + (1.0 - keep) * mine[...]
        if level + 1 < LEVELS:
            leaf_start(level)
            broadcast(level)

    gather_plane(final, mine[...], LEVELS - 1)
    for q in range(nx):
        out_ref[:, pl.ds(q * quarter, quarter), :] = final[q]

    if fast:
        wait_bytes(flags.at[pl.ds(0, nl - 1)], need_recv.at[2])
        flag = flags[0]
        for node in range(1, nl):
            flag = jnp.maximum(flag, flags[node])
        flag_ref[...] = flag
    else:
        flag_ref[...] = jnp.zeros_like(flag_ref)
    drain_part(LEVELS - 1)
    for ref, sem in drains:
        wait_bytes(ref, sem)


def call(cap, rhs_t, diag_inverse, tiles, block_rows, block_cols, block_count, node_level):
    per_node, columns, width = rhs_t.shape
    slots = tiles.shape[0]
    nl, nb = lax.axis_size("leaf"), lax.axis_size("blk")
    nz = per_node
    nx = nb // nz
    quarter = columns // nx
    half = quarter // 2
    last = LEVELS - 1
    fast = cap == 0
    dma = pltpu.SemaphoreType.DMA
    hbm = pl.BlockSpec(memory_space=pltpu.HBM)
    vmem = pltpu.VMEM
    smem = pltpu.SMEM
    whole = pl.BlockSpec(memory_space=pltpu.VMEM)
    box = (nx, nz, quarter, width) if fast else (2, nx, nz, cap, half, width)
    side = (nl, quarter, width) if fast else (nl, half, width)
    return pl.pallas_call(
        functools.partial(kernel, cap, nl, nz, nx, slots, quarter, width),
        out_shape=(
            jax.ShapeDtypeStruct((per_node, columns, width), F32),
            jax.ShapeDtypeStruct((8, width), F32),
        ),
        in_specs=[hbm] * 7,
        out_specs=(whole, whole),
        scratch_shapes=[
            smem(node_level.shape, jnp.int32),
            smem(block_rows.shape, jnp.int32),
            smem(block_cols.shape, jnp.int32),
            smem(block_count.shape, jnp.int32),
            vmem((slots, width, width), F32),
            vmem((width, width), F32),
            vmem((quarter, width), F32),
            vmem((slots, width, 2 * width), BF16),
            vmem((slots, columns, width), F32),
            vmem((nx, nz, quarter, width), F32),
            vmem((last, nx - 1, nz, quarter, width), F32),
            vmem((last, nz, quarter, width), F32),
            vmem((last, nz - 1, quarter, width), F32),
            vmem((LEVELS, quarter, width), F32),
            vmem((nl, half, width), F32),
            vmem(side, F32),
            vmem(side, F32),
            vmem((2, nx, nz, 1, half, width), F32),
            vmem(box, F32),
            vmem(box, F32),
            vmem((nx, nz, quarter, width), F32),
            vmem((quarter, width), F32),
            vmem((8, width), F32),
            vmem((nz - 1, 8, width), F32),
            vmem((nx - 1, 8, width), F32),
            vmem((nl, 8, width), F32),
            smem((nl,), jnp.int32),
            smem((last * max(cap, 1),), jnp.int32),
            smem((slots,), jnp.int32),
            smem((slots,), jnp.int32),
            dma((7,)),
            dma((last,)),
            dma((last,)),
            dma((last,)),
            dma((last,)),
            dma((last,)),
            dma((last,)),
            dma((LEVELS,)),
            dma((LEVELS,)),
            dma((LEVELS,)),
            dma((LEVELS, nx - 1)),
            dma((last,)),
            dma((last,)),
            dma((3,)),
            dma((3,)),
        ],
        compiler_params=pltpu.CompilerParams(
            collective_id=0 if fast else 1, has_side_effects=True, vmem_limit_bytes=VMEM_LIMIT
        ),
        name="tree_solve" if fast else "tree_solve_listed",
    )(node_level, block_rows, block_cols, block_count, rhs_t, diag_inverse, tiles)


def body(adjoint_rhs, diag_inverse, blocks, block_rows, block_cols, block_count, node_level):
    args = (
        jnp.swapaxes(adjoint_rhs, 1, 2), diag_inverse, blocks.reshape(blocks.shape[2:]),
        block_rows, block_cols, block_count, node_level,
    )
    solved, flag = call(0, *args)
    cap = lax.axis_size("leaf") - 3
    solved = lax.cond(flag[0, 0] > 0.5, lambda: call(cap, *args)[0], lambda: solved)
    return jnp.swapaxes(solved, 1, 2)


def solution(mesh):
    in_specs = (
        P("leaf", None, None),
        P("leaf", None, None),
        P("leaf", "blk", None, None, None),
        P("leaf", "blk", None),
        P("leaf", "blk", None),
        P("leaf", "blk"),
        P(),
    )
    out_specs = P("leaf", None, None)
    return jax.shard_map(body, mesh=mesh, in_specs=in_specs, out_specs=out_specs, check_vma=False)
```

```python
import functools

import jax
import jax.numpy as jnp
from jax import lax
from jax.experimental import pallas as pl
from jax.experimental.pallas import tpu as pltpu
from jax.sharding import PartitionSpec as P

LEVELS = 4
VMEM_LIMIT = 60 * 1024 * 1024
MESH = pl.DeviceIdType.MESH
F32 = jnp.float32
BF16 = jnp.bfloat16


def split(value):
    high = value.astype(BF16)
    return high, (value - high.astype(F32)).astype(BF16)


def kernel(
    cap, nl, nz, nx, slots, quarter, width,
    level_hbm, rows_hbm, cols_hbm, count_hbm, rhs_hbm, dinv_hbm, tiles_hbm,
    out_ref, flag_ref,
    level_ref, rows_ref, cols_ref, count_ref,
    tiles, dinv, own_rhs, weights, prods, part, from_plane, piece, leaf0, leaf1, leaf2, gather0, gather1, gather2,
    final, mine, need, need_z, need_x, flags, rank, names, slot_node, slot_level,
    local_sems, leaf_send, leaf_recv, part_send, part_recv, agz_send, agz_recv, agx_send, agx_recv,
    core_send, core_recv, need_send, need_recv,
):
    fast = cap == 0
    half = quarter // 2
    leaf, blk = lax.axis_index("leaf"), lax.axis_index("blk")
    core = lax.rem(leaf, 2)
    z, x = lax.div(blk, nx), lax.rem(blk, nx)
    gathers = (gather0, gather1, gather2)
    from_leaf = (leaf0, leaf1, leaf2)

    def z_peer(k):
        return lax.rem(z + k, nz)

    def x_peer(k):
        return lax.rem(x + k, nx)

    def at_z(k):
        return (leaf, z_peer(k) * nx + x)

    def at_x(k):
        return (leaf, z * nx + x_peer(k))

    def at_leaf(k):
        return (lax.rem(leaf + k, nl), blk)

    sibling = (leaf + 1 - 2 * core, blk)

    barrier = pltpu.get_barrier_semaphore()
    partners = [at_leaf(k) for k in range(1, nl)] + [at_z(k) for k in range(1, nz)] + [at_x(k) for k in range(1, nx)]
    for partner in partners:
        pl.semaphore_signal(barrier, inc=1, device_id=partner, device_id_type=MESH)

    copies = [
        pltpu.make_async_copy(dinv_hbm.at[z], dinv, local_sems.at[0]),
        pltpu.make_async_copy(
            rhs_hbm.at[z, pl.ds(pl.multiple_of(x * quarter, 8), quarter)], own_rhs, local_sems.at[1]
        ),
        pltpu.make_async_copy(level_hbm, level_ref, local_sems.at[2]),
        pltpu.make_async_copy(rows_hbm, rows_ref, local_sems.at[3]),
        pltpu.make_async_copy(cols_hbm, cols_ref, local_sems.at[4]),
        pltpu.make_async_copy(count_hbm, count_ref, local_sems.at[5]),
        pltpu.make_async_copy(tiles_hbm, tiles, local_sems.at[6]),
    ]
    for copy in copies:
        copy.start()

    def solve(summed):
        return lax.dot_general(
            own_rhs[...] - summed, dinv[...], (((1,), (1,)), ((), ())),
            precision=lax.Precision.HIGHEST, preferred_element_type=F32,
        )

    copies[0].wait()
    copies[1].wait()
    piece[0] = solve(jnp.zeros((quarter, width), F32))
    mine[...] = piece[0]
    for copy in copies[2:6]:
        copy.wait()

    if fast:
        root = jnp.int32(0)
        for node in range(nl):
            root = jnp.maximum(root, jnp.where(level_ref[node] == 0, node, 0))
        names[0] = root
    else:
        for node in range(nl):
            at = jnp.int32(0)
            for other in range(node):
                at = at + jnp.where(level_ref[other] == level_ref[node], 1, 0)
            rank[node] = at
        for level in range(LEVELS - 1):
            for j in range(1 if level == 0 else cap):
                name = jnp.int32(0)
                for node in range(nl):
                    name = name + jnp.where((level_ref[node] == level) & (rank[node] == j), node, 0)
                names[level * cap + j] = name

    def read_slot(s, seen):
        node = lax.div(rows_ref[0, 0, s], nz)
        level = jnp.where(s < count_ref[0, 0], level_ref[node], -1)
        slot_level[s] = level
        if not fast:
            slot_node[s] = jnp.minimum(rank[node], cap - 1)
        top1, low1, top2, low2 = seen
        return (
            jnp.maximum(top1, jnp.where(level == 1, node, -1)),
            jnp.maximum(low1, jnp.where(level == 1, -node, -nl)),
            jnp.maximum(top2, jnp.where(level == 2, node, -1)),
            jnp.maximum(low2, jnp.where(level == 2, -node, -nl)),
        )

    first = (jnp.int32(-1), jnp.int32(-nl), jnp.int32(-1), jnp.int32(-nl))
    seen = lax.fori_loop(0, slots, read_slot, first)
    my_level = level_ref[leaf]
    pl.semaphore_wait(barrier, len(partners))

    def wait_bytes(ref, sem):
        pltpu.make_async_copy(ref, ref, sem).wait()

    drains = []

    def send(src, dst, send_sem, recv_sem, device):
        pltpu.make_async_remote_copy(
            src_ref=src, dst_ref=dst, send_sem=send_sem, recv_sem=recv_sem, device_id=device, device_id_type=MESH
        ).start()

    def halves(level):
        return level == 0 or not fast

    leaf_order = [nl // 2 + (-1) ** i * ((i + 1) // 2) for i in range(nl - 1)]

    def leaf_start(level):
        for k in leaf_order:
            peer = at_leaf(k)
            rows = pl.ds(pl.multiple_of(lax.rem(peer[0], 2) * half, 8), half)
            src = piece.at[level, rows] if halves(level) else piece.at[level]
            send(src, from_leaf[level].at[leaf], leaf_send.at[level], leaf_recv.at[level], peer)
        if halves(level):
            from_leaf[level][leaf] = piece[level, pl.ds(pl.multiple_of(core * half, 8), half), :]
        else:
            from_leaf[level][leaf] = piece[level]
        drains.append((from_leaf[level].at[pl.ds(0, nl - 1)], leaf_send.at[level]))

    def far_first(i, n):
        step = lax.div(i + 1, 2)
        return jnp.where(lax.rem(i, 2) == 1, n // 2 - step, n // 2 + step)

    def plane_loop(visit):
        order = [nx // 2 + (-1) ** i * ((i + 1) // 2) for i in range(nx)]

        def one(i, _):
            dz = far_first(i, nz)
            visit(dz, order)
            return 0

        lax.fori_loop(0, nz - 1, one, 0)
        visit(0, [dx for dx in order if dx])

    def send_all(own, box_at, send_sem, recv_sem):
        def visit(dz, order):
            for dx in order:
                send(own, box_at, send_sem, recv_sem, (leaf, z_peer(dz) * nx + x_peer(dx)))

        plane_loop(visit)

    def gather_plane(box, level):
        own = box.at[blk]
        send_all(own, own, agz_send.at[level], agz_recv.at[level])
        others = box.at[pl.ds(0, nz * nx - 1)]
        wait_bytes(others, agz_recv.at[level])
        drains.append((others, agz_send.at[level]))

    def broadcast_root():
        box = gather0
        wait_bytes(leaf0.at[pl.ds(0, nl - 1)], leaf_recv.at[0])
        need_across()
        box[core, blk] = leaf0[names[0]]
        side = box.at[core]
        gather_plane(side, 0)
        send(side, side, core_send.at[0], core_recv.at[0], sibling)
        wait_bytes(side, core_recv.at[0])
        drains.append((side, core_send.at[0]))

    def broadcast_listed(level):
        box = gathers[level]
        for j in range(cap):
            box[core, x, z, j] = from_leaf[level][names[level * cap + j]]
        own = box.at[core, x, z]
        for k in range(1, nz):
            send(own, own, agz_send.at[level], agz_recv.at[level], at_z(k))
        wait_bytes(box.at[core, x, pl.ds(0, nz - 1)], agz_recv.at[level])
        line = box.at[core, x]
        for k in range(1, nx):
            send(line, line, agx_send.at[level], agx_recv.at[level, k - 1], at_x(k))
        send(line, line, core_send.at[level], core_recv.at[level], sibling)
        for k in range(1, nx):
            wait_bytes(line, agx_recv.at[level, k - 1])
            got = box.at[core, lax.rem(x + nx - k, nx)]
            send(got, got, core_send.at[level], core_recv.at[level], sibling)
        wait_bytes(box.at[core], core_recv.at[level])
        drains.append((box.at[0, 0, pl.ds(0, nz - 1)], agz_send.at[level]))
        drains.append((box.at[0, pl.ds(0, nx - 1)], agx_send.at[level]))
        drains.append((box.at[0], core_send.at[level]))

    def broadcast(level):
        wait_bytes(from_leaf[level].at[pl.ds(0, nl - 1)], leaf_recv.at[level])
        if not fast:
            broadcast_listed(level)
            return
        wanted = need[2 * level - 2 : 2 * level - 1, :]
        chosen = jnp.zeros((quarter, width), F32)
        for node in range(nl):
            chosen = jnp.where(wanted == float(node), from_leaf[level][node], chosen)
        gathers[level][blk] = chosen
        gather_plane(gathers[level], level)

    def need_start():
        at = lax.broadcasted_iota(jnp.int32, (8, width), 0)
        tile = jnp.full((8, width), -float(nl), F32)
        for i, value in enumerate(seen):
            tile = jnp.where(at == i, value.astype(F32), tile)
        need[...] = tile
        for k in range(1, nz):
            send(need, need_z.at[k - 1], need_send.at[0], need_recv.at[0], at_z(k))

    def need_across():
        wait_bytes(need_z, need_recv.at[0])
        wait_bytes(need_z, need_send.at[0])
        tile = need[...]
        for k in range(nz - 1):
            tile = jnp.maximum(tile, need_z[k])
        need[...] = tile
        for k in range(1, nx):
            send(need, need_x.at[k - 1], need_send.at[1], need_recv.at[1], at_x(k))

    def need_end():
        wait_bytes(need_x, need_recv.at[1])
        wait_bytes(need_x, need_send.at[1])
        tile = need[...]
        for k in range(nx - 1):
            tile = jnp.maximum(tile, need_x[k])
        need[...] = tile
        several = (tile[0:1] + tile[1:2] > 0.0) | (tile[2:3] + tile[3:4] > 0.0)
        flags[leaf] = jnp.where(jnp.broadcast_to(several, (8, width)), 1.0, 0.0).astype(F32)
        for k in range(1, nl):
            send(flags.at[leaf], flags.at[leaf], need_send.at[2], need_recv.at[2], at_leaf(k))
        drains.append((flags.at[pl.ds(0, nl - 1)], need_send.at[2]))

    def products(level):
        box = gathers[level - 1]

        def one(s, _):
            at = lax.rem(rows_ref[0, 0, s], nz)
            if level == 1:
                panel = jnp.concatenate([box[h, at * nx + q] for q in range(nx) for h in range(2)], axis=0)
            elif fast:
                panel = jnp.concatenate([box[at * nx + q] for q in range(nx)], axis=0)
            else:
                node = slot_node[s]
                panel = jnp.concatenate([box[h, q, at, node] for q in range(nx) for h in range(2)], axis=0)
            high, low = split(panel)
            both = jnp.concatenate([high, low], axis=0)
            got = jnp.dot(both, weights[s], preferred_element_type=F32)
            n = nx * quarter
            prods[s] = (got[:n, width:] + got[n:, :width]) + got[:n, :width]
            return 0

        lax.fori_loop(0, slots, one, 0, unroll=4)

        def column(c):
            total = jnp.zeros((nx * quarter, width), F32)
            for s in range(slots):
                key = jnp.where(slot_level[s] == level - 1, cols_ref[0, 0, s], -1)
                total = total + jnp.where(key == c, 1.0, 0.0).astype(F32) * prods[s]
            for q in range(nx):
                mass = total[q * quarter : (q + 1) * quarter]
                part[q, c] = mass if level == 1 else part[q, c] + mass

        def visit(dz, order):
            c = z_peer(dz)
            column(c)
            for dx in order:
                send(
                    part.at[x_peer(dx), c], from_plane.at[level - 1, dz * nx + dx],
                    part_send.at[level - 1], part_recv.at[level - 1], (leaf, c * nx + x_peer(dx)),
                )

        plane_loop(visit)

    def reduce(level):
        at = level - 1
        if level == 1:
            need_end()
        wait_bytes(from_plane.at[at, pl.ds(1, nz * nx - 1)], part_recv.at[at])
        total = part[x, z]
        for k in range(1, nz * nx):
            total = total + from_plane[at, k]
        return total

    def drain_part(level):
        wait_bytes(from_plane.at[level - 1, pl.ds(1, nz * nx - 1)], part_send.at[level - 1])

    leaf_start(0)
    need_start()
    copies[6].wait()

    def prepare(s, _):
        high, low = split(tiles[s])
        weights[s, :, :width] = high
        weights[s, :, width:] = low
        return 0

    lax.fori_loop(0, slots, prepare, 0, unroll=2)
    broadcast_root()
    for level in range(1, LEVELS):
        if level > 1:
            drain_part(level - 1)
        products(level)
        solved = solve(reduce(level))
        piece[level] = solved
        keep = jnp.where(my_level == level, 1.0, 0.0).astype(F32)
        mine[...] = keep * solved + (1.0 - keep) * mine[...]
        if level + 1 < LEVELS:
            leaf_start(level)
            broadcast(level)

    final[blk] = mine[...]
    gather_plane(final, LEVELS - 1)
    for q in range(nx):
        for c in range(nz):
            out_ref[c, pl.ds(q * quarter, quarter), :] = final[c * nx + q]

    wait_bytes(flags.at[pl.ds(0, nl - 1)], need_recv.at[2])
    flag = flags[0]
    for node in range(1, nl):
        flag = jnp.maximum(flag, flags[node])
    flag_ref[0, 0] = jnp.where(jnp.max(flag) > 0.5, 1, 0).astype(jnp.int32)
    drain_part(LEVELS - 1)
    for ref, sem in drains:
        wait_bytes(ref, sem)


def call(cap, rhs_t, diag_inverse, tiles, block_rows, block_cols, block_count, node_level):
    per_node, columns, width = rhs_t.shape
    slots = tiles.shape[0]
    nl, nb = lax.axis_size("leaf"), lax.axis_size("blk")
    nz = per_node
    nx = nb // nz
    quarter = columns // nx
    half = quarter // 2
    last = LEVELS - 1
    fast = cap == 0
    dma = pltpu.SemaphoreType.DMA
    hbm = pl.BlockSpec(memory_space=pltpu.HBM)
    vmem = pltpu.VMEM
    smem = pltpu.SMEM
    whole = pl.BlockSpec(memory_space=pltpu.VMEM)
    box = (nb, quarter, width) if fast else (2, nx, nz, cap, half, width)
    side = (nl, quarter, width) if fast else (nl, half, width)
    return pl.pallas_call(
        functools.partial(kernel, cap, nl, nz, nx, slots, quarter, width),
        out_shape=(
            jax.ShapeDtypeStruct((per_node, columns, width), F32),
            jax.ShapeDtypeStruct((1, 1), jnp.int32),
        ),
        in_specs=[hbm] * 7,
        out_specs=(whole, pl.BlockSpec(memory_space=pltpu.SMEM)),
        scratch_shapes=[
            smem(node_level.shape, jnp.int32),
            smem(block_rows.shape, jnp.int32),
            smem(block_cols.shape, jnp.int32),
            smem(block_count.shape, jnp.int32),
            vmem((slots, width, width), F32),
            vmem((width, width), F32),
            vmem((quarter, width), F32),
            vmem((slots, width, 2 * width), BF16),
            vmem((slots, columns, width), F32),
            vmem((nx, nz, quarter, width), F32),
            vmem((last, nb, quarter, width), F32),
            vmem((LEVELS, quarter, width), F32),
            vmem((nl, half, width), F32),
            vmem(side, F32),
            vmem(side, F32),
            vmem((2, nb, half, width), F32),
            vmem(box, F32),
            vmem(box, F32),
            vmem((nb, quarter, width), F32),
            vmem((quarter, width), F32),
            vmem((8, width), F32),
            vmem((nz - 1, 8, width), F32),
            vmem((nx - 1, 8, width), F32),
            vmem((nl, 8, width), F32),
            smem((nl,), jnp.int32),
            smem((last * max(cap, 1),), jnp.int32),
            smem((slots,), jnp.int32),
            smem((slots,), jnp.int32),
            dma((7,)),
            dma((last,)),
            dma((last,)),
            dma((last,)),
            dma((last,)),
            dma((LEVELS,)),
            dma((LEVELS,)),
            dma((LEVELS,)),
            dma((LEVELS, nx - 1)),
            dma((last,)),
            dma((last,)),
            dma((3,)),
            dma((3,)),
        ],
        compiler_params=pltpu.CompilerParams(
            collective_id=0 if fast else 1, has_side_effects=True, vmem_limit_bytes=VMEM_LIMIT
        ),
        name="tree_solve" if fast else "tree_solve_listed",
    )(node_level, block_rows, block_cols, block_count, rhs_t, diag_inverse, tiles)


def body(adjoint_rhs, diag_inverse, blocks, block_rows, block_cols, block_count, node_level):
    args = (
        jnp.swapaxes(adjoint_rhs, 1, 2), diag_inverse, blocks.reshape(blocks.shape[2:]),
        block_rows, block_cols, block_count, node_level,
    )
    solved, flag = call(0, *args)
    cap = lax.axis_size("leaf") - 3
    solved = lax.cond(flag[0, 0] > 0, lambda: call(cap, *args)[0], lambda: solved)
    return jnp.swapaxes(solved, 1, 2)


def solution(mesh):
    in_specs = (
        P("leaf", None, None),
        P("leaf", None, None),
        P("leaf", "blk", None, None, None),
        P("leaf", "blk", None),
        P("leaf", "blk", None),
        P("leaf", "blk"),
        P(),
    )
    out_specs = P("leaf", None, None)
    return jax.shard_map(body, mesh=mesh, in_specs=in_specs, out_specs=out_specs, check_vma=False)
```

```python
import functools

import jax
import jax.numpy as jnp
from jax import lax
from jax.experimental import pallas as pl
from jax.experimental.pallas import tpu as pltpu
from jax.sharding import PartitionSpec as P

LEVELS = 4
UNROLL = 8
VMEM_LIMIT = 60 * 1024 * 1024
MESH = pl.DeviceIdType.MESH
F32 = jnp.float32
BF16 = jnp.bfloat16


def split(value):
    high = value.astype(BF16)
    return high, (value - high.astype(F32)).astype(BF16)


def kernel(
    cap, nl, nz, nx, slots, quarter, width,
    level_hbm, rows_hbm, cols_hbm, count_hbm, rhs_hbm, dinv_hbm, tiles_hbm,
    out_ref, flag_ref,
    level_ref, rows_ref, cols_ref, count_ref,
    tiles, dinv, own_rhs, weights, panels, prods, part, from_plane, piece, leaf0, leaf1, leaf2, gather0, gather1, gather2,
    final, mine, need, need_z, need_x, flags, rank, names, slot_node, slot_level,
    local_sems, leaf_send, leaf_recv, part_send, part_recv, agz_send, agz_recv, agx_send, agx_recv,
    core_send, core_recv, need_send, need_recv,
):
    fast = cap == 0
    half = quarter // 2
    leaf, blk = lax.axis_index("leaf"), lax.axis_index("blk")
    core = lax.rem(leaf, 2)
    z, x = lax.div(blk, nx), lax.rem(blk, nx)
    gathers = (gather0, gather1, gather2)
    from_leaf = (leaf0, leaf1, leaf2)

    def z_peer(k):
        return lax.rem(z + k, nz)

    def x_peer(k):
        return lax.rem(x + k, nx)

    def at_z(k):
        return (leaf, z_peer(k) * nx + x)

    def at_x(k):
        return (leaf, z * nx + x_peer(k))

    def at_leaf(k):
        return (lax.rem(leaf + k, nl), blk)

    sibling = (leaf + 1 - 2 * core, blk)

    barrier = pltpu.get_barrier_semaphore()
    partners = [at_leaf(k) for k in range(1, nl)] + [at_z(k) for k in range(1, nz)] + [at_x(k) for k in range(1, nx)]
    for partner in partners:
        pl.semaphore_signal(barrier, inc=1, device_id=partner, device_id_type=MESH)

    copies = [
        pltpu.make_async_copy(dinv_hbm.at[z], dinv, local_sems.at[0]),
        pltpu.make_async_copy(
            rhs_hbm.at[z, pl.ds(pl.multiple_of(x * quarter, 8), quarter)], own_rhs, local_sems.at[1]
        ),
        pltpu.make_async_copy(level_hbm, level_ref, local_sems.at[2]),
        pltpu.make_async_copy(rows_hbm, rows_ref, local_sems.at[3]),
        pltpu.make_async_copy(cols_hbm, cols_ref, local_sems.at[4]),
        pltpu.make_async_copy(count_hbm, count_ref, local_sems.at[5]),
        pltpu.make_async_copy(tiles_hbm, tiles, local_sems.at[6]),
    ]
    for copy in copies:
        copy.start()

    def solve(summed):
        return lax.dot_general(
            own_rhs[...] - summed, dinv[...], (((1,), (1,)), ((), ())),
            precision=lax.Precision.HIGHEST, preferred_element_type=F32,
        )

    copies[0].wait()
    copies[1].wait()
    piece[0] = solve(jnp.zeros((quarter, width), F32))
    mine[...] = piece[0]
    for copy in copies[2:6]:
        copy.wait()

    if fast:
        root = jnp.int32(0)
        for node in range(nl):
            root = jnp.maximum(root, jnp.where(level_ref[node] == 0, node, 0))
        names[0] = root
    else:
        for node in range(nl):
            at = jnp.int32(0)
            for other in range(node):
                at = at + jnp.where(level_ref[other] == level_ref[node], 1, 0)
            rank[node] = at
        for level in range(LEVELS - 1):
            for j in range(1 if level == 0 else cap):
                name = jnp.int32(0)
                for node in range(nl):
                    name = name + jnp.where((level_ref[node] == level) & (rank[node] == j), node, 0)
                names[level * cap + j] = name

    def read_slot(s, seen):
        node = lax.div(rows_ref[0, 0, s], nz)
        level = jnp.where(s < count_ref[0, 0], level_ref[node], -1)
        slot_level[s] = level
        if not fast:
            slot_node[s] = jnp.minimum(rank[node], cap - 1)
        top1, low1, top2, low2 = seen
        return (
            jnp.maximum(top1, jnp.where(level == 1, node, -1)),
            jnp.maximum(low1, jnp.where(level == 1, -node, -nl)),
            jnp.maximum(top2, jnp.where(level == 2, node, -1)),
            jnp.maximum(low2, jnp.where(level == 2, -node, -nl)),
        )

    first = (jnp.int32(-1), jnp.int32(-nl), jnp.int32(-1), jnp.int32(-nl))
    seen = lax.fori_loop(0, slots, read_slot, first)
    my_level = level_ref[leaf]
    pl.semaphore_wait(barrier, len(partners))

    def wait_bytes(ref, sem):
        pltpu.make_async_copy(ref, ref, sem).wait()

    drains = []

    def send(src, dst, send_sem, recv_sem, device):
        pltpu.make_async_remote_copy(
            src_ref=src, dst_ref=dst, send_sem=send_sem, recv_sem=recv_sem, device_id=device, device_id_type=MESH
        ).start()

    def halves(level):
        return level == 0 or not fast

    leaf_order = [nl // 2 + (-1) ** i * ((i + 1) // 2) for i in range(nl - 1)]

    def leaf_start(level):
        for k in leaf_order:
            peer = at_leaf(k)
            rows = pl.ds(pl.multiple_of(lax.rem(peer[0], 2) * half, 8), half)
            src = piece.at[level, rows] if halves(level) else piece.at[level]
            send(src, from_leaf[level].at[leaf], leaf_send.at[level], leaf_recv.at[level], peer)
        if halves(level):
            from_leaf[level][leaf] = piece[level, pl.ds(pl.multiple_of(core * half, 8), half), :]
        else:
            from_leaf[level][leaf] = piece[level]
        drains.append((from_leaf[level].at[pl.ds(0, nl - 1)], leaf_send.at[level]))

    def far_first(i, n):
        step = lax.div(i + 1, 2)
        return jnp.where(lax.rem(i, 2) == 1, n // 2 - step, n // 2 + step)

    def plane_loop(visit):
        order = [nx // 2 + (-1) ** i * ((i + 1) // 2) for i in range(nx)]

        def one(i, _):
            dz = far_first(i, nz)
            visit(dz, order)
            return 0

        lax.fori_loop(0, nz - 1, one, 0)
        visit(0, [dx for dx in order if dx])

    def send_all(own, box_at, send_sem, recv_sem):
        def visit(dz, order):
            for dx in order:
                send(own, box_at, send_sem, recv_sem, (leaf, z_peer(dz) * nx + x_peer(dx)))

        plane_loop(visit)

    def gather_plane(box, level):
        own = box.at[blk]
        send_all(own, own, agz_send.at[level], agz_recv.at[level])
        others = box.at[pl.ds(0, nz * nx - 1)]
        wait_bytes(others, agz_recv.at[level])
        drains.append((others, agz_send.at[level]))

    def broadcast_root():
        box = gather0
        wait_bytes(leaf0.at[pl.ds(0, nl - 1)], leaf_recv.at[0])
        need_across()
        box[core, blk] = leaf0[names[0]]
        side = box.at[core]
        gather_plane(side, 0)
        send(side, side, core_send.at[0], core_recv.at[0], sibling)
        wait_bytes(side, core_recv.at[0])
        drains.append((side, core_send.at[0]))

    def broadcast_listed(level):
        box = gathers[level]
        for j in range(cap):
            box[core, x, z, j] = from_leaf[level][names[level * cap + j]]
        own = box.at[core, x, z]
        for k in range(1, nz):
            send(own, own, agz_send.at[level], agz_recv.at[level], at_z(k))
        wait_bytes(box.at[core, x, pl.ds(0, nz - 1)], agz_recv.at[level])
        line = box.at[core, x]
        for k in range(1, nx):
            send(line, line, agx_send.at[level], agx_recv.at[level, k - 1], at_x(k))
        send(line, line, core_send.at[level], core_recv.at[level], sibling)
        for k in range(1, nx):
            wait_bytes(line, agx_recv.at[level, k - 1])
            got = box.at[core, lax.rem(x + nx - k, nx)]
            send(got, got, core_send.at[level], core_recv.at[level], sibling)
        wait_bytes(box.at[core], core_recv.at[level])
        drains.append((box.at[0, 0, pl.ds(0, nz - 1)], agz_send.at[level]))
        drains.append((box.at[0, pl.ds(0, nx - 1)], agx_send.at[level]))
        drains.append((box.at[0], core_send.at[level]))

    def broadcast(level):
        wait_bytes(from_leaf[level].at[pl.ds(0, nl - 1)], leaf_recv.at[level])
        if not fast:
            broadcast_listed(level)
            return
        wanted = need[2 * level - 2 : 2 * level - 1, :]
        chosen = jnp.zeros((quarter, width), F32)
        for node in range(nl):
            chosen = jnp.where(wanted == float(node), from_leaf[level][node], chosen)
        gathers[level][blk] = chosen
        gather_plane(gathers[level], level)

    def need_start():
        at = lax.broadcasted_iota(jnp.int32, (8, width), 0)
        tile = jnp.full((8, width), -float(nl), F32)
        for i, value in enumerate(seen):
            tile = jnp.where(at == i, value.astype(F32), tile)
        need[...] = tile
        for k in range(1, nz):
            send(need, need_z.at[k - 1], need_send.at[0], need_recv.at[0], at_z(k))

    def need_across():
        wait_bytes(need_z, need_recv.at[0])
        wait_bytes(need_z, need_send.at[0])
        tile = need[...]
        for k in range(nz - 1):
            tile = jnp.maximum(tile, need_z[k])
        need[...] = tile
        for k in range(1, nx):
            send(need, need_x.at[k - 1], need_send.at[1], need_recv.at[1], at_x(k))

    def need_end():
        wait_bytes(need_x, need_recv.at[1])
        wait_bytes(need_x, need_send.at[1])
        tile = need[...]
        for k in range(nx - 1):
            tile = jnp.maximum(tile, need_x[k])
        need[...] = tile
        several = (tile[0:1] + tile[1:2] > 0.0) | (tile[2:3] + tile[3:4] > 0.0)
        flags[leaf] = jnp.where(jnp.broadcast_to(several, (8, width)), 1.0, 0.0).astype(F32)
        for k in range(1, nl):
            send(flags.at[leaf], flags.at[leaf], need_send.at[2], need_recv.at[2], at_leaf(k))
        drains.append((flags.at[pl.ds(0, nl - 1)], need_send.at[2]))

    def products(level):
        box = gathers[level - 1]

        listed = cap if level > 1 and not fast else 1

        def arrange(c, _):
            for node in range(listed):
                for q in range(nx):
                    if level == 1:
                        panel = jnp.concatenate([box[h, c * nx + q] for h in range(2)], axis=0)
                    elif fast:
                        panel = box[c * nx + q]
                    else:
                        panel = jnp.concatenate([box[h, q, c, node] for h in range(2)], axis=0)
                    high, low = split(panel)
                    rows = pl.ds(q * quarter, quarter)
                    panels[c * listed + node, rows, pl.ds(0, width)] = high
                    panels[c * listed + node, rows, pl.ds(width, width)] = low
            return 0

        lax.fori_loop(0, nz, arrange, 0, unroll=True if listed == 1 else 1)

        def one(s, _):
            at = lax.rem(rows_ref[0, 0, s], nz)
            if listed > 1:
                at = at * listed + slot_node[s]
            got = jnp.dot(panels[at], weights[s], preferred_element_type=F32)
            prods[s] = got[:, width:] + got[:, :width]
            return 0

        lax.fori_loop(0, slots, one, 0, unroll=UNROLL)

        def column(c):
            total = jnp.zeros((nx * quarter, width), F32)
            for s in range(slots):
                key = jnp.where(slot_level[s] == level - 1, cols_ref[0, 0, s], -1)
                total = total + jnp.where(key == c, 1.0, 0.0).astype(F32) * prods[s]
            for q in range(nx):
                mass = total[q * quarter : (q + 1) * quarter]
                part[q, c] = mass if level == 1 else part[q, c] + mass

        def visit(dz, order):
            c = z_peer(dz)
            column(c)
            for dx in order:
                send(
                    part.at[x_peer(dx), c], from_plane.at[level - 1, dz * nx + dx],
                    part_send.at[level - 1], part_recv.at[level - 1], (leaf, c * nx + x_peer(dx)),
                )

        plane_loop(visit)

    def reduce(level):
        at = level - 1
        if level == 1:
            need_end()
        wait_bytes(from_plane.at[at, pl.ds(1, nz * nx - 1)], part_recv.at[at])
        total = part[x, z]
        for k in range(1, nz * nx):
            total = total + from_plane[at, k]
        return total

    def drain_part(level):
        wait_bytes(from_plane.at[level - 1, pl.ds(1, nz * nx - 1)], part_send.at[level - 1])

    leaf_start(0)
    need_start()
    copies[6].wait()

    def prepare(s, _):
        high, low = split(tiles[s])
        weights[s, :width, :width] = high
        weights[s, :width, width:] = low
        weights[s, width:, :width] = high
        weights[s, width:, width:] = jnp.zeros_like(low)
        return 0

    lax.fori_loop(0, slots, prepare, 0, unroll=2)
    broadcast_root()
    for level in range(1, LEVELS):
        if level > 1:
            drain_part(level - 1)
        products(level)
        solved = solve(reduce(level))
        piece[level] = solved
        keep = jnp.where(my_level == level, 1.0, 0.0).astype(F32)
        mine[...] = keep * solved + (1.0 - keep) * mine[...]
        if level + 1 < LEVELS:
            leaf_start(level)
            broadcast(level)

    final[blk] = mine[...]
    gather_plane(final, LEVELS - 1)
    for q in range(nx):
        for c in range(nz):
            out_ref[c, pl.ds(q * quarter, quarter), :] = final[c * nx + q]

    wait_bytes(flags.at[pl.ds(0, nl - 1)], need_recv.at[2])
    flag = flags[0]
    for node in range(1, nl):
        flag = jnp.maximum(flag, flags[node])
    flag_ref[0, 0] = jnp.where(jnp.max(flag) > 0.5, 1, 0).astype(jnp.int32)
    drain_part(LEVELS - 1)
    for ref, sem in drains:
        wait_bytes(ref, sem)


def call(cap, rhs_t, diag_inverse, tiles, block_rows, block_cols, block_count, node_level):
    per_node, columns, width = rhs_t.shape
    slots = tiles.shape[0]
    nl, nb = lax.axis_size("leaf"), lax.axis_size("blk")
    nz = per_node
    nx = nb // nz
    quarter = columns // nx
    half = quarter // 2
    last = LEVELS - 1
    fast = cap == 0
    dma = pltpu.SemaphoreType.DMA
    hbm = pl.BlockSpec(memory_space=pltpu.HBM)
    vmem = pltpu.VMEM
    smem = pltpu.SMEM
    whole = pl.BlockSpec(memory_space=pltpu.VMEM)
    box = (nb, quarter, width) if fast else (2, nx, nz, cap, half, width)
    side = (nl, quarter, width) if fast else (nl, half, width)
    return pl.pallas_call(
        functools.partial(kernel, cap, nl, nz, nx, slots, quarter, width),
        out_shape=(
            jax.ShapeDtypeStruct((per_node, columns, width), F32),
            jax.ShapeDtypeStruct((1, 1), jnp.int32),
        ),
        in_specs=[hbm] * 7,
        out_specs=(whole, pl.BlockSpec(memory_space=pltpu.SMEM)),
        scratch_shapes=[
            smem(node_level.shape, jnp.int32),
            smem(block_rows.shape, jnp.int32),
            smem(block_cols.shape, jnp.int32),
            smem(block_count.shape, jnp.int32),
            vmem((slots, width, width), F32),
            vmem((width, width), F32),
            vmem((quarter, width), F32),
            vmem((slots, 2 * width, 2 * width), BF16),
            vmem((nz * (1 if fast else cap), columns, 2 * width), BF16),
            vmem((slots, columns, width), F32),
            vmem((nx, nz, quarter, width), F32),
            vmem((last, nb, quarter, width), F32),
            vmem((LEVELS, quarter, width), F32),
            vmem((nl, half, width), F32),
            vmem(side, F32),
            vmem(side, F32),
            vmem((2, nb, half, width), F32),
            vmem(box, F32),
            vmem(box, F32),
            vmem((nb, quarter, width), F32),
            vmem((quarter, width), F32),
            vmem((8, width), F32),
            vmem((nz - 1, 8, width), F32),
            vmem((nx - 1, 8, width), F32),
            vmem((nl, 8, width), F32),
            smem((nl,), jnp.int32),
            smem((last * max(cap, 1),), jnp.int32),
            smem((slots,), jnp.int32),
            smem((slots,), jnp.int32),
            dma((7,)),
            dma((last,)),
            dma((last,)),
            dma((last,)),
            dma((last,)),
            dma((LEVELS,)),
            dma((LEVELS,)),
            dma((LEVELS,)),
            dma((LEVELS, nx - 1)),
            dma((last,)),
            dma((last,)),
            dma((3,)),
            dma((3,)),
        ],
        compiler_params=pltpu.CompilerParams(
            collective_id=0 if fast else 1, has_side_effects=True, vmem_limit_bytes=VMEM_LIMIT
        ),
        name="tree_solve" if fast else "tree_solve_listed",
    )(node_level, block_rows, block_cols, block_count, rhs_t, diag_inverse, tiles)


def body(adjoint_rhs, diag_inverse, blocks, block_rows, block_cols, block_count, node_level):
    args = (
        jnp.swapaxes(adjoint_rhs, 1, 2), diag_inverse, blocks.reshape(blocks.shape[2:]),
        block_rows, block_cols, block_count, node_level,
    )
    solved, flag = call(0, *args)
    cap = lax.axis_size("leaf") - 3
    solved = lax.cond(flag[0, 0] > 0, lambda: call(cap, *args)[0], lambda: solved)
    return jnp.swapaxes(solved, 1, 2)


def solution(mesh):
    in_specs = (
        P("leaf", None, None),
        P("leaf", None, None),
        P("leaf", "blk", None, None, None),
        P("leaf", "blk", None),
        P("leaf", "blk", None),
        P("leaf", "blk"),
        P(),
    )
    out_specs = P("leaf", None, None)
    return jax.shard_map(body, mesh=mesh, in_specs=in_specs, out_specs=out_specs, check_vma=False)
```

```python
import functools

import jax
import jax.numpy as jnp
from jax import lax
from jax.experimental import pallas as pl
from jax.experimental.pallas import tpu as pltpu
from jax.sharding import PartitionSpec as P

LEVELS = 4
UNROLL = 8
VMEM_LIMIT = 60 * 1024 * 1024
MESH = pl.DeviceIdType.MESH
F32 = jnp.float32
BF16 = jnp.bfloat16


def split(value):
    high = value.astype(BF16)
    return high, (value - high.astype(F32)).astype(BF16)


def kernel(
    cap, nl, nz, nx, slots, quarter, width,
    level_hbm, rows_hbm, cols_hbm, count_hbm, rhs_hbm, dinv_hbm, tiles_hbm,
    out_ref, flag_ref,
    level_ref, rows_ref, cols_ref, count_ref,
    tiles, dinv, own_rhs, weights, panels, prods, part, from_plane, piece, leaf0, leaf1, leaf2, gather0, gather1, gather2,
    final, mine, need, need_z, need_x, flags, rank, names, slot_node, slot_level,
    local_sems, leaf_send, leaf_recv, part_send, part_recv, agz_send, agz_recv, agx_send, agx_recv,
    core_send, core_recv, need_send, need_recv,
):
    fast = cap == 0
    half = quarter // 2
    leaf, blk = lax.axis_index("leaf"), lax.axis_index("blk")
    core = lax.rem(leaf, 2)
    z, x = lax.div(blk, nx), lax.rem(blk, nx)
    gathers = (gather0, gather1, gather2)
    from_leaf = (leaf0, leaf1, leaf2)

    def z_peer(k):
        return lax.rem(z + k, nz)

    def x_peer(k):
        return lax.rem(x + k, nx)

    def at_z(k):
        return (leaf, z_peer(k) * nx + x)

    def at_x(k):
        return (leaf, z * nx + x_peer(k))

    def at_leaf(k):
        return (lax.rem(leaf + k, nl), blk)

    sibling = (leaf + 1 - 2 * core, blk)

    barrier = pltpu.get_barrier_semaphore()
    partners = [at_leaf(k) for k in range(1, nl)] + [at_z(k) for k in range(1, nz)] + [at_x(k) for k in range(1, nx)]
    for partner in partners:
        pl.semaphore_signal(barrier, inc=1, device_id=partner, device_id_type=MESH)

    copies = [
        pltpu.make_async_copy(dinv_hbm.at[z], dinv, local_sems.at[0]),
        pltpu.make_async_copy(
            rhs_hbm.at[z, pl.ds(pl.multiple_of(x * quarter, 8), quarter)], own_rhs, local_sems.at[1]
        ),
        pltpu.make_async_copy(level_hbm, level_ref, local_sems.at[2]),
        pltpu.make_async_copy(rows_hbm, rows_ref, local_sems.at[3]),
        pltpu.make_async_copy(cols_hbm, cols_ref, local_sems.at[4]),
        pltpu.make_async_copy(count_hbm, count_ref, local_sems.at[5]),
        pltpu.make_async_copy(tiles_hbm, tiles, local_sems.at[6]),
    ]
    for copy in copies:
        copy.start()

    def solve(summed):
        return lax.dot_general(
            own_rhs[...] - summed, dinv[...], (((1,), (1,)), ((), ())),
            precision=lax.Precision.HIGHEST, preferred_element_type=F32,
        )

    copies[0].wait()
    copies[1].wait()
    piece[0] = solve(jnp.zeros((quarter, width), F32))
    mine[...] = piece[0]
    for copy in copies[2:6]:
        copy.wait()

    if fast:
        root = jnp.int32(0)
        for node in range(nl):
            root = jnp.maximum(root, jnp.where(level_ref[node] == 0, node, 0))
        names[0] = root
    else:
        for node in range(nl):
            at = jnp.int32(0)
            for other in range(node):
                at = at + jnp.where(level_ref[other] == level_ref[node], 1, 0)
            rank[node] = at
        for level in range(LEVELS - 1):
            for j in range(1 if level == 0 else cap):
                name = jnp.int32(0)
                for node in range(nl):
                    name = name + jnp.where((level_ref[node] == level) & (rank[node] == j), node, 0)
                names[level * cap + j] = name

    def read_slot(s, seen):
        node = lax.div(rows_ref[0, 0, s], nz)
        level = jnp.where(s < count_ref[0, 0], level_ref[node], -1)
        slot_level[s] = level
        if not fast:
            slot_node[s] = jnp.minimum(rank[node], cap - 1)
        top1, low1, top2, low2 = seen
        return (
            jnp.maximum(top1, jnp.where(level == 1, node, -1)),
            jnp.maximum(low1, jnp.where(level == 1, -node, -nl)),
            jnp.maximum(top2, jnp.where(level == 2, node, -1)),
            jnp.maximum(low2, jnp.where(level == 2, -node, -nl)),
        )

    first = (jnp.int32(-1), jnp.int32(-nl), jnp.int32(-1), jnp.int32(-nl))
    seen = lax.fori_loop(0, slots, read_slot, first)
    my_level = level_ref[leaf]
    pl.semaphore_wait(barrier, len(partners))

    def wait_bytes(ref, sem):
        pltpu.make_async_copy(ref, ref, sem).wait()

    drains = []

    def send(src, dst, send_sem, recv_sem, device):
        pltpu.make_async_remote_copy(
            src_ref=src, dst_ref=dst, send_sem=send_sem, recv_sem=recv_sem, device_id=device, device_id_type=MESH
        ).start()

    def halves(level):
        return level == 0 or not fast

    leaf_order = [nl // 2 + (-1) ** i * ((i + 1) // 2) for i in range(nl - 1)]

    def leaf_start(level):
        for k in leaf_order:
            peer = at_leaf(k)
            rows = pl.ds(pl.multiple_of(lax.rem(peer[0], 2) * half, 8), half)
            src = piece.at[level, rows] if halves(level) else piece.at[level]
            send(src, from_leaf[level].at[leaf], leaf_send.at[level], leaf_recv.at[level], peer)
        if halves(level):
            from_leaf[level][leaf] = piece[level, pl.ds(pl.multiple_of(core * half, 8), half), :]
        else:
            from_leaf[level][leaf] = piece[level]
        drains.append((from_leaf[level].at[pl.ds(0, nl - 1)], leaf_send.at[level]))

    def far_first(i, n):
        step = lax.div(i + 1, 2)
        return jnp.where(lax.rem(i, 2) == 1, lax.rem(n // 2 + step, n), n // 2 - step)

    def plane_loop(visit):
        order = [nx // 2 + (-1) ** i * ((i + 1) // 2) for i in range(nx)]

        def one(i, _):
            dz = far_first(i, nz)
            visit(dz, order)
            return 0

        lax.fori_loop(0, nz - 1, one, 0)
        visit(0, [dx for dx in order if dx])

    def send_all(own, box_at, send_sem, recv_sem):
        def visit(dz, order):
            for dx in order:
                send(own, box_at, send_sem, recv_sem, (leaf, z_peer(dz) * nx + x_peer(dx)))

        def far(n, d):
            return min(d, n - d)

        pairs = [(a, b) for a in range(nz) for b in range(nx) if a or b]
        for dz, dx in sorted(pairs, key=lambda p: (-far(nz, p[0]) - far(nx, p[1]), -far(nz, p[0]), -p[0])):
            visit(dz, [dx])

    def gather_plane(box, level):
        own = box.at[blk]
        send_all(own, own, agz_send.at[level], agz_recv.at[level])
        others = box.at[pl.ds(0, nz * nx - 1)]
        wait_bytes(others, agz_recv.at[level])
        drains.append((others, agz_send.at[level]))

    def broadcast_root():
        box = gather0
        wait_bytes(leaf0.at[pl.ds(0, nl - 1)], leaf_recv.at[0])
        need_across()
        box[core, blk] = leaf0[names[0]]
        side = box.at[core]
        gather_plane(side, 0)
        send(side, side, core_send.at[0], core_recv.at[0], sibling)
        wait_bytes(side, core_recv.at[0])
        drains.append((side, core_send.at[0]))

    def broadcast_listed(level):
        box = gathers[level]
        for j in range(cap):
            box[core, x, z, j] = from_leaf[level][names[level * cap + j]]
        own = box.at[core, x, z]
        for k in range(1, nz):
            send(own, own, agz_send.at[level], agz_recv.at[level], at_z(k))
        wait_bytes(box.at[core, x, pl.ds(0, nz - 1)], agz_recv.at[level])
        line = box.at[core, x]
        for k in range(1, nx):
            send(line, line, agx_send.at[level], agx_recv.at[level, k - 1], at_x(k))
        send(line, line, core_send.at[level], core_recv.at[level], sibling)
        for k in range(1, nx):
            wait_bytes(line, agx_recv.at[level, k - 1])
            got = box.at[core, lax.rem(x + nx - k, nx)]
            send(got, got, core_send.at[level], core_recv.at[level], sibling)
        wait_bytes(box.at[core], core_recv.at[level])
        drains.append((box.at[0, 0, pl.ds(0, nz - 1)], agz_send.at[level]))
        drains.append((box.at[0, pl.ds(0, nx - 1)], agx_send.at[level]))
        drains.append((box.at[0], core_send.at[level]))

    def broadcast(level):
        wait_bytes(from_leaf[level].at[pl.ds(0, nl - 1)], leaf_recv.at[level])
        if not fast:
            broadcast_listed(level)
            return
        wanted = need[2 * level - 2 : 2 * level - 1, :]
        chosen = jnp.zeros((quarter, width), F32)
        for node in range(nl):
            chosen = jnp.where(wanted == float(node), from_leaf[level][node], chosen)
        gathers[level][blk] = chosen
        gather_plane(gathers[level], level)

    def need_start():
        at = lax.broadcasted_iota(jnp.int32, (8, width), 0)
        tile = jnp.full((8, width), -float(nl), F32)
        for i, value in enumerate(seen):
            tile = jnp.where(at == i, value.astype(F32), tile)
        need[...] = tile
        for k in range(1, nz):
            send(need, need_z.at[k - 1], need_send.at[0], need_recv.at[0], at_z(k))

    def need_across():
        wait_bytes(need_z, need_recv.at[0])
        wait_bytes(need_z, need_send.at[0])
        tile = need[...]
        for k in range(nz - 1):
            tile = jnp.maximum(tile, need_z[k])
        need[...] = tile
        for k in range(1, nx):
            send(need, need_x.at[k - 1], need_send.at[1], need_recv.at[1], at_x(k))

    def need_end():
        wait_bytes(need_x, need_recv.at[1])
        wait_bytes(need_x, need_send.at[1])
        tile = need[...]
        for k in range(nx - 1):
            tile = jnp.maximum(tile, need_x[k])
        need[...] = tile
        several = (tile[0:1] + tile[1:2] > 0.0) | (tile[2:3] + tile[3:4] > 0.0)
        flags[leaf] = jnp.where(jnp.broadcast_to(several, (8, width)), 1.0, 0.0).astype(F32)
        for k in range(1, nl):
            send(flags.at[leaf], flags.at[leaf], need_send.at[2], need_recv.at[2], at_leaf(k))
        drains.append((flags.at[pl.ds(0, nl - 1)], need_send.at[2]))

    def products(level):
        box = gathers[level - 1]

        listed = cap if level > 1 and not fast else 1

        def arrange(c, _):
            for node in range(listed):
                for q in range(nx):
                    if level == 1:
                        panel = jnp.concatenate([box[h, c * nx + q] for h in range(2)], axis=0)
                    elif fast:
                        panel = box[c * nx + q]
                    else:
                        panel = jnp.concatenate([box[h, q, c, node] for h in range(2)], axis=0)
                    high, low = split(panel)
                    rows = pl.ds(q * quarter, quarter)
                    panels[c * listed + node, rows, pl.ds(0, width)] = high
                    panels[c * listed + node, rows, pl.ds(width, width)] = low
            return 0

        lax.fori_loop(0, nz, arrange, 0, unroll=True if listed == 1 else 1)

        def one(s, _):
            at = lax.rem(rows_ref[0, 0, s], nz)
            if listed > 1:
                at = at * listed + slot_node[s]
            got = jnp.dot(panels[at], weights[s], preferred_element_type=F32)
            prods[s] = got[:, width:] + got[:, :width]
            return 0

        lax.fori_loop(0, slots, one, 0, unroll=UNROLL)

        def column(c):
            total = jnp.zeros((nx * quarter, width), F32)
            for s in range(slots):
                key = jnp.where(slot_level[s] == level - 1, cols_ref[0, 0, s], -1)
                total = total + jnp.where(key == c, 1.0, 0.0).astype(F32) * prods[s]
            for q in range(nx):
                mass = total[q * quarter : (q + 1) * quarter]
                part[q, c] = mass if level == 1 else part[q, c] + mass

        def visit(dz, order):
            c = z_peer(dz)
            column(c)
            for dx in order:
                send(
                    part.at[x_peer(dx), c], from_plane.at[level - 1, dz * nx + dx],
                    part_send.at[level - 1], part_recv.at[level - 1], (leaf, c * nx + x_peer(dx)),
                )

        plane_loop(visit)

    def reduce(level):
        at = level - 1
        if level == 1:
            need_end()
        wait_bytes(from_plane.at[at, pl.ds(1, nz * nx - 1)], part_recv.at[at])
        total = part[x, z]
        for k in range(1, nz * nx):
            total = total + from_plane[at, k]
        return total

    def drain_part(level):
        wait_bytes(from_plane.at[level - 1, pl.ds(1, nz * nx - 1)], part_send.at[level - 1])

    leaf_start(0)
    need_start()
    copies[6].wait()

    def prepare(s, _):
        high, low = split(tiles[s])
        weights[s, :width, :width] = high
        weights[s, :width, width:] = low
        weights[s, width:, :width] = high
        weights[s, width:, width:] = jnp.zeros_like(low)
        return 0

    lax.fori_loop(0, slots, prepare, 0, unroll=2)
    broadcast_root()
    for level in range(1, LEVELS):
        if level > 1:
            drain_part(level - 1)
        products(level)
        solved = solve(reduce(level))
        piece[level] = solved
        keep = jnp.where(my_level == level, 1.0, 0.0).astype(F32)
        mine[...] = keep * solved + (1.0 - keep) * mine[...]
        if level + 1 < LEVELS:
            leaf_start(level)
            broadcast(level)

    final[blk] = mine[...]
    gather_plane(final, LEVELS - 1)
    for q in range(nx):
        for c in range(nz):
            out_ref[c, pl.ds(q * quarter, quarter), :] = final[c * nx + q]

    wait_bytes(flags.at[pl.ds(0, nl - 1)], need_recv.at[2])
    flag = flags[0]
    for node in range(1, nl):
        flag = jnp.maximum(flag, flags[node])
    flag_ref[0, 0] = jnp.where(jnp.max(flag) > 0.5, 1, 0).astype(jnp.int32)
    drain_part(LEVELS - 1)
    for ref, sem in drains:
        wait_bytes(ref, sem)


def call(cap, rhs_t, diag_inverse, tiles, block_rows, block_cols, block_count, node_level):
    per_node, columns, width = rhs_t.shape
    slots = tiles.shape[0]
    nl, nb = lax.axis_size("leaf"), lax.axis_size("blk")
    nz = per_node
    nx = nb // nz
    quarter = columns // nx
    half = quarter // 2
    last = LEVELS - 1
    fast = cap == 0
    dma = pltpu.SemaphoreType.DMA
    hbm = pl.BlockSpec(memory_space=pltpu.HBM)
    vmem = pltpu.VMEM
    smem = pltpu.SMEM
    whole = pl.BlockSpec(memory_space=pltpu.VMEM)
    box = (nb, quarter, width) if fast else (2, nx, nz, cap, half, width)
    side = (nl, quarter, width) if fast else (nl, half, width)
    return pl.pallas_call(
        functools.partial(kernel, cap, nl, nz, nx, slots, quarter, width),
        out_shape=(
            jax.ShapeDtypeStruct((per_node, columns, width), F32),
            jax.ShapeDtypeStruct((1, 1), jnp.int32),
        ),
        in_specs=[hbm] * 7,
        out_specs=(whole, pl.BlockSpec(memory_space=pltpu.SMEM)),
        scratch_shapes=[
            smem(node_level.shape, jnp.int32),
            smem(block_rows.shape, jnp.int32),
            smem(block_cols.shape, jnp.int32),
            smem(block_count.shape, jnp.int32),
            vmem((slots, width, width), F32),
            vmem((width, width), F32),
            vmem((quarter, width), F32),
            vmem((slots, 2 * width, 2 * width), BF16),
            vmem((nz * (1 if fast else cap), columns, 2 * width), BF16),
            vmem((slots, columns, width), F32),
            vmem((nx, nz, quarter, width), F32),
            vmem((last, nb, quarter, width), F32),
            vmem((LEVELS, quarter, width), F32),
            vmem((nl, half, width), F32),
            vmem(side, F32),
            vmem(side, F32),
            vmem((2, nb, half, width), F32),
            vmem(box, F32),
            vmem(box, F32),
            vmem((nb, quarter, width), F32),
            vmem((quarter, width), F32),
            vmem((8, width), F32),
            vmem((nz - 1, 8, width), F32),
            vmem((nx - 1, 8, width), F32),
            vmem((nl, 8, width), F32),
            smem((nl,), jnp.int32),
            smem((last * max(cap, 1),), jnp.int32),
            smem((slots,), jnp.int32),
            smem((slots,), jnp.int32),
            dma((7,)),
            dma((last,)),
            dma((last,)),
            dma((last,)),
            dma((last,)),
            dma((LEVELS,)),
            dma((LEVELS,)),
            dma((LEVELS,)),
            dma((LEVELS, nx - 1)),
            dma((last,)),
            dma((last,)),
            dma((3,)),
            dma((3,)),
        ],
        compiler_params=pltpu.CompilerParams(
            collective_id=0 if fast else 1, has_side_effects=True, vmem_limit_bytes=VMEM_LIMIT
        ),
        name="tree_solve" if fast else "tree_solve_listed",
    )(node_level, block_rows, block_cols, block_count, rhs_t, diag_inverse, tiles)


def body(adjoint_rhs, diag_inverse, blocks, block_rows, block_cols, block_count, node_level):
    args = (
        jnp.swapaxes(adjoint_rhs, 1, 2), diag_inverse, blocks.reshape(blocks.shape[2:]),
        block_rows, block_cols, block_count, node_level,
    )
    solved, flag = call(0, *args)
    cap = lax.axis_size("leaf") - 3
    solved = lax.cond(flag[0, 0] > 0, lambda: call(cap, *args)[0], lambda: solved)
    return jnp.swapaxes(solved, 1, 2)


def solution(mesh):
    in_specs = (
        P("leaf", None, None),
        P("leaf", None, None),
        P("leaf", "blk", None, None, None),
        P("leaf", "blk", None),
        P("leaf", "blk", None),
        P("leaf", "blk"),
        P(),
    )
    out_specs = P("leaf", None, None)
    return jax.shard_map(body, mesh=mesh, in_specs=in_specs, out_specs=out_specs, check_vma=False)
```

```python
import functools

import jax
import jax.numpy as jnp
from jax import lax
from jax.experimental import pallas as pl
from jax.experimental.pallas import tpu as pltpu
from jax.sharding import PartitionSpec as P

LEVELS = 4
UNROLL = 8
VMEM_LIMIT = 60 * 1024 * 1024
MESH = pl.DeviceIdType.MESH
F32 = jnp.float32
BF16 = jnp.bfloat16


def split(value):
    high = value.astype(BF16)
    return high, (value - high.astype(F32)).astype(BF16)


def kernel(
    cap, nl, nz, nx, slots, quarter, width,
    level_hbm, rows_hbm, cols_hbm, count_hbm, rhs_hbm, dinv_hbm, tiles_hbm,
    out_ref, flag_ref,
    level_ref, rows_ref, cols_ref, count_ref,
    tiles, dinv, inverse, own_rhs, weights, panels, prods, part, from_plane, piece, leaf0, leaf1, leaf2, gather0, gather1, gather2,
    final, mine, need, need_z, need_x, flags, rank, names, slot_node, slot_level,
    local_sems, leaf_send, leaf_recv, part_send, part_recv, agz_send, agz_recv, agx_send, agx_recv,
    core_send, core_recv, need_send, need_recv,
):
    fast = cap == 0
    half = quarter // 2
    leaf, blk = lax.axis_index("leaf"), lax.axis_index("blk")
    core = lax.rem(leaf, 2)
    z, x = lax.div(blk, nx), lax.rem(blk, nx)
    gathers = (gather0, gather1, gather2)
    from_leaf = (leaf0, leaf1, leaf2)

    def z_peer(k):
        return lax.rem(z + k, nz)

    def x_peer(k):
        return lax.rem(x + k, nx)

    def at_z(k):
        return (leaf, z_peer(k) * nx + x)

    def at_x(k):
        return (leaf, z * nx + x_peer(k))

    def at_leaf(k):
        return (lax.rem(leaf + k, nl), blk)

    sibling = (leaf + 1 - 2 * core, blk)

    barrier = pltpu.get_barrier_semaphore()
    partners = [at_leaf(k) for k in range(1, nl)] + [at_z(k) for k in range(1, nz)] + [at_x(k) for k in range(1, nx)]
    for partner in partners:
        pl.semaphore_signal(barrier, inc=1, device_id=partner, device_id_type=MESH)

    copies = [
        pltpu.make_async_copy(dinv_hbm.at[z], dinv, local_sems.at[0]),
        pltpu.make_async_copy(
            rhs_hbm.at[z, pl.ds(pl.multiple_of(x * quarter, 8), quarter)], own_rhs, local_sems.at[1]
        ),
        pltpu.make_async_copy(level_hbm, level_ref, local_sems.at[2]),
        pltpu.make_async_copy(rows_hbm, rows_ref, local_sems.at[3]),
        pltpu.make_async_copy(cols_hbm, cols_ref, local_sems.at[4]),
        pltpu.make_async_copy(count_hbm, count_ref, local_sems.at[5]),
        pltpu.make_async_copy(tiles_hbm, tiles, local_sems.at[6]),
    ]
    for copy in copies:
        copy.start()

    def fill(ref, matrix):
        high, low = split(matrix)
        ref[:width, :width] = high
        ref[:width, width:] = low
        ref[width:, :width] = high
        ref[width:, width:] = jnp.zeros_like(low)

    def solve(summed):
        both = jnp.concatenate(split(own_rhs[...] - summed), axis=1)
        got = jnp.dot(both, inverse[...], preferred_element_type=F32)
        return got[:, width:] + got[:, :width]

    copies[0].wait()
    fill(inverse, dinv[...].T)
    copies[1].wait()
    piece[0] = solve(jnp.zeros((quarter, width), F32))
    mine[...] = piece[0]
    for copy in copies[2:6]:
        copy.wait()

    if fast:
        root = jnp.int32(0)
        for node in range(nl):
            root = jnp.maximum(root, jnp.where(level_ref[node] == 0, node, 0))
        names[0] = root
    else:
        for node in range(nl):
            at = jnp.int32(0)
            for other in range(node):
                at = at + jnp.where(level_ref[other] == level_ref[node], 1, 0)
            rank[node] = at
        for level in range(LEVELS - 1):
            for j in range(1 if level == 0 else cap):
                name = jnp.int32(0)
                for node in range(nl):
                    name = name + jnp.where((level_ref[node] == level) & (rank[node] == j), node, 0)
                names[level * cap + j] = name

    def read_slot(s, seen):
        node = lax.div(rows_ref[0, 0, s], nz)
        level = jnp.where(s < count_ref[0, 0], level_ref[node], -1)
        slot_level[s] = level
        if not fast:
            slot_node[s] = jnp.minimum(rank[node], cap - 1)
        top1, low1, top2, low2 = seen
        return (
            jnp.maximum(top1, jnp.where(level == 1, node, -1)),
            jnp.maximum(low1, jnp.where(level == 1, -node, -nl)),
            jnp.maximum(top2, jnp.where(level == 2, node, -1)),
            jnp.maximum(low2, jnp.where(level == 2, -node, -nl)),
        )

    first = (jnp.int32(-1), jnp.int32(-nl), jnp.int32(-1), jnp.int32(-nl))
    seen = lax.fori_loop(0, slots, read_slot, first)
    my_level = level_ref[leaf]
    pl.semaphore_wait(barrier, len(partners))

    def wait_bytes(ref, sem):
        pltpu.make_async_copy(ref, ref, sem).wait()

    drains = []

    def send(src, dst, send_sem, recv_sem, device):
        pltpu.make_async_remote_copy(
            src_ref=src, dst_ref=dst, send_sem=send_sem, recv_sem=recv_sem, device_id=device, device_id_type=MESH
        ).start()

    def halves(level):
        return level == 0 or not fast

    leaf_order = [nl // 2 + (-1) ** i * ((i + 1) // 2) for i in range(nl - 1)]

    def leaf_start(level):
        for k in leaf_order:
            peer = at_leaf(k)
            rows = pl.ds(pl.multiple_of(lax.rem(peer[0], 2) * half, 8), half)
            src = piece.at[level, rows] if halves(level) else piece.at[level]
            send(src, from_leaf[level].at[leaf], leaf_send.at[level], leaf_recv.at[level], peer)
        if halves(level):
            from_leaf[level][leaf] = piece[level, pl.ds(pl.multiple_of(core * half, 8), half), :]
        else:
            from_leaf[level][leaf] = piece[level]
        drains.append((from_leaf[level].at[pl.ds(0, nl - 1)], leaf_send.at[level]))

    def far_first(i, n):
        step = lax.div(i + 1, 2)
        return jnp.where(lax.rem(i, 2) == 1, lax.rem(n // 2 + step, n), n // 2 - step)

    def plane_loop(visit):
        order = [nx // 2 + (-1) ** i * ((i + 1) // 2) for i in range(nx)]

        def one(i, _):
            dz = far_first(i, nz)
            visit(dz, order)
            return 0

        lax.fori_loop(0, nz - 1, one, 0)
        visit(0, [dx for dx in order if dx])

    def send_all(own, box_at, send_sem, recv_sem):
        def visit(dz, order):
            for dx in order:
                send(own, box_at, send_sem, recv_sem, (leaf, z_peer(dz) * nx + x_peer(dx)))

        def far(n, d):
            return min(d, n - d)

        pairs = [(a, b) for a in range(nz) for b in range(nx) if a or b]
        for dz, dx in sorted(pairs, key=lambda p: (-far(nz, p[0]) - far(nx, p[1]), -far(nz, p[0]), -p[0])):
            visit(dz, [dx])

    def gather_plane(box, level, meanwhile=None):
        own = box.at[blk]
        send_all(own, own, agz_send.at[level], agz_recv.at[level])
        if meanwhile:
            meanwhile()
        others = box.at[pl.ds(0, nz * nx - 1)]
        wait_bytes(others, agz_recv.at[level])
        drains.append((others, agz_send.at[level]))

    def broadcast_root():
        box = gather0
        wait_bytes(leaf0.at[pl.ds(0, nl - 1)], leaf_recv.at[0])
        wait_bytes(need_z, need_recv.at[0])
        box[core, blk] = leaf0[names[0]]
        side = box.at[core]
        gather_plane(side, 0, need_across)
        send(side, side, core_send.at[0], core_recv.at[0], sibling)
        wait_bytes(side, core_recv.at[0])
        drains.append((side, core_send.at[0]))

    def broadcast_listed(level):
        box = gathers[level]
        for j in range(cap):
            box[core, x, z, j] = from_leaf[level][names[level * cap + j]]
        own = box.at[core, x, z]
        for k in range(1, nz):
            send(own, own, agz_send.at[level], agz_recv.at[level], at_z(k))
        wait_bytes(box.at[core, x, pl.ds(0, nz - 1)], agz_recv.at[level])
        line = box.at[core, x]
        for k in range(1, nx):
            send(line, line, agx_send.at[level], agx_recv.at[level, k - 1], at_x(k))
        send(line, line, core_send.at[level], core_recv.at[level], sibling)
        for k in range(1, nx):
            wait_bytes(line, agx_recv.at[level, k - 1])
            got = box.at[core, lax.rem(x + nx - k, nx)]
            send(got, got, core_send.at[level], core_recv.at[level], sibling)
        wait_bytes(box.at[core], core_recv.at[level])
        drains.append((box.at[0, 0, pl.ds(0, nz - 1)], agz_send.at[level]))
        drains.append((box.at[0, pl.ds(0, nx - 1)], agx_send.at[level]))
        drains.append((box.at[0], core_send.at[level]))

    def broadcast(level):
        wait_bytes(from_leaf[level].at[pl.ds(0, nl - 1)], leaf_recv.at[level])
        if not fast:
            broadcast_listed(level)
            return
        wanted = need[2 * level - 2 : 2 * level - 1, :]
        chosen = jnp.zeros((quarter, width), F32)
        for node in range(nl):
            chosen = jnp.where(wanted == float(node), from_leaf[level][node], chosen)
        gathers[level][blk] = chosen
        gather_plane(gathers[level], level)

    def need_start():
        at = lax.broadcasted_iota(jnp.int32, (8, width), 0)
        tile = jnp.full((8, width), -float(nl), F32)
        for i, value in enumerate(seen):
            tile = jnp.where(at == i, value.astype(F32), tile)
        need[...] = tile
        for k in range(1, nz):
            send(need, need_z.at[k - 1], need_send.at[0], need_recv.at[0], at_z(k))

    def need_across():
        wait_bytes(need_z, need_send.at[0])
        tile = need[...]
        for k in range(nz - 1):
            tile = jnp.maximum(tile, need_z[k])
        need[...] = tile
        for k in range(1, nx):
            send(need, need_x.at[k - 1], need_send.at[1], need_recv.at[1], at_x(k))

    def need_end():
        wait_bytes(need_x, need_recv.at[1])
        wait_bytes(need_x, need_send.at[1])
        tile = need[...]
        for k in range(nx - 1):
            tile = jnp.maximum(tile, need_x[k])
        need[...] = tile
        several = (tile[0:1] + tile[1:2] > 0.0) | (tile[2:3] + tile[3:4] > 0.0)
        flags[leaf] = jnp.where(jnp.broadcast_to(several, (8, width)), 1.0, 0.0).astype(F32)
        for k in range(1, nl):
            send(flags.at[leaf], flags.at[leaf], need_send.at[2], need_recv.at[2], at_leaf(k))
        drains.append((flags.at[pl.ds(0, nl - 1)], need_send.at[2]))

    def products(level):
        box = gathers[level - 1]

        listed = cap if level > 1 and not fast else 1

        def arrange(c, _):
            for node in range(listed):
                for q in range(nx):
                    if level == 1:
                        panel = jnp.concatenate([box[h, c * nx + q] for h in range(2)], axis=0)
                    elif fast:
                        panel = box[c * nx + q]
                    else:
                        panel = jnp.concatenate([box[h, q, c, node] for h in range(2)], axis=0)
                    high, low = split(panel)
                    rows = pl.ds(q * quarter, quarter)
                    panels[c * listed + node, rows, pl.ds(0, width)] = high
                    panels[c * listed + node, rows, pl.ds(width, width)] = low
            return 0

        lax.fori_loop(0, nz, arrange, 0, unroll=True if listed == 1 else 1)

        def one(s, _):
            at = lax.rem(rows_ref[0, 0, s], nz)
            if listed > 1:
                at = at * listed + slot_node[s]
            got = jnp.dot(panels[at], weights[s], preferred_element_type=F32)
            prods[s] = got[:, width:] + got[:, :width]
            return 0

        lax.fori_loop(0, slots, one, 0, unroll=UNROLL)

        def column(c):
            total = jnp.zeros((nx * quarter, width), F32)
            for s in range(slots):
                key = jnp.where(slot_level[s] == level - 1, cols_ref[0, 0, s], -1)
                total = total + jnp.where(key == c, 1.0, 0.0).astype(F32) * prods[s]
            for q in range(nx):
                mass = total[q * quarter : (q + 1) * quarter]
                part[q, c] = mass if level == 1 else part[q, c] + mass

        def visit(dz, order):
            c = z_peer(dz)
            column(c)
            for dx in order:
                send(
                    part.at[x_peer(dx), c], from_plane.at[level - 1, dz * nx + dx],
                    part_send.at[level - 1], part_recv.at[level - 1], (leaf, c * nx + x_peer(dx)),
                )

        plane_loop(visit)

    def reduce(level):
        at = level - 1
        if level == 1:
            need_end()
        wait_bytes(from_plane.at[at, pl.ds(1, nz * nx - 1)], part_recv.at[at])
        total = part[x, z]
        for k in range(1, nz * nx):
            total = total + from_plane[at, k]
        return total

    def drain_part(level):
        wait_bytes(from_plane.at[level - 1, pl.ds(1, nz * nx - 1)], part_send.at[level - 1])

    leaf_start(0)
    need_start()
    copies[6].wait()

    def prepare(s, _):
        high, low = split(tiles[s])
        weights[s, :width, :width] = high
        weights[s, :width, width:] = low
        weights[s, width:, :width] = high
        weights[s, width:, width:] = jnp.zeros_like(low)
        return 0

    lax.fori_loop(0, slots, prepare, 0, unroll=2)
    broadcast_root()
    for level in range(1, LEVELS):
        if level > 1:
            drain_part(level - 1)
        products(level)
        solved = solve(reduce(level))
        piece[level] = solved
        keep = jnp.where(my_level == level, 1.0, 0.0).astype(F32)
        mine[...] = keep * solved + (1.0 - keep) * mine[...]
        if level + 1 < LEVELS:
            leaf_start(level)
            broadcast(level)

    final[blk] = mine[...]
    gather_plane(final, LEVELS - 1)
    for q in range(nx):
        for c in range(nz):
            out_ref[c, pl.ds(q * quarter, quarter), :] = final[c * nx + q]

    wait_bytes(flags.at[pl.ds(0, nl - 1)], need_recv.at[2])
    flag = flags[0]
    for node in range(1, nl):
        flag = jnp.maximum(flag, flags[node])
    flag_ref[0, 0] = jnp.where(jnp.max(flag) > 0.5, 1, 0).astype(jnp.int32)
    drain_part(LEVELS - 1)
    for ref, sem in drains:
        wait_bytes(ref, sem)


def call(cap, rhs_t, diag_inverse, tiles, block_rows, block_cols, block_count, node_level):
    per_node, columns, width = rhs_t.shape
    slots = tiles.shape[0]
    nl, nb = lax.axis_size("leaf"), lax.axis_size("blk")
    nz = per_node
    nx = nb // nz
    quarter = columns // nx
    half = quarter // 2
    last = LEVELS - 1
    fast = cap == 0
    dma = pltpu.SemaphoreType.DMA
    hbm = pl.BlockSpec(memory_space=pltpu.HBM)
    vmem = pltpu.VMEM
    smem = pltpu.SMEM
    whole = pl.BlockSpec(memory_space=pltpu.VMEM)
    box = (nb, quarter, width) if fast else (2, nx, nz, cap, half, width)
    side = (nl, quarter, width) if fast else (nl, half, width)
    return pl.pallas_call(
        functools.partial(kernel, cap, nl, nz, nx, slots, quarter, width),
        out_shape=(
            jax.ShapeDtypeStruct((per_node, columns, width), F32),
            jax.ShapeDtypeStruct((1, 1), jnp.int32),
        ),
        in_specs=[hbm] * 7,
        out_specs=(whole, pl.BlockSpec(memory_space=pltpu.SMEM)),
        scratch_shapes=[
            smem(node_level.shape, jnp.int32),
            smem(block_rows.shape, jnp.int32),
            smem(block_cols.shape, jnp.int32),
            smem(block_count.shape, jnp.int32),
            vmem((slots, width, width), F32),
            vmem((width, width), F32),
            vmem((2 * width, 2 * width), BF16),
            vmem((quarter, width), F32),
            vmem((slots, 2 * width, 2 * width), BF16),
            vmem((nz * (1 if fast else cap), columns, 2 * width), BF16),
            vmem((slots, columns, width), F32),
            vmem((nx, nz, quarter, width), F32),
            vmem((last, nb, quarter, width), F32),
            vmem((LEVELS, quarter, width), F32),
            vmem((nl, half, width), F32),
            vmem(side, F32),
            vmem(side, F32),
            vmem((2, nb, half, width), F32),
            vmem(box, F32),
            vmem(box, F32),
            vmem((nb, quarter, width), F32),
            vmem((quarter, width), F32),
            vmem((8, width), F32),
            vmem((nz - 1, 8, width), F32),
            vmem((nx - 1, 8, width), F32),
            vmem((nl, 8, width), F32),
            smem((nl,), jnp.int32),
            smem((last * max(cap, 1),), jnp.int32),
            smem((slots,), jnp.int32),
            smem((slots,), jnp.int32),
            dma((7,)),
            dma((last,)),
            dma((last,)),
            dma((last,)),
            dma((last,)),
            dma((LEVELS,)),
            dma((LEVELS,)),
            dma((LEVELS,)),
            dma((LEVELS, nx - 1)),
            dma((last,)),
            dma((last,)),
            dma((3,)),
            dma((3,)),
        ],
        compiler_params=pltpu.CompilerParams(
            collective_id=0 if fast else 1, has_side_effects=True, vmem_limit_bytes=VMEM_LIMIT
        ),
        name="tree_solve" if fast else "tree_solve_listed",
    )(node_level, block_rows, block_cols, block_count, rhs_t, diag_inverse, tiles)


def body(adjoint_rhs, diag_inverse, blocks, block_rows, block_cols, block_count, node_level):
    args = (
        jnp.swapaxes(adjoint_rhs, 1, 2), diag_inverse, blocks.reshape(blocks.shape[2:]),
        block_rows, block_cols, block_count, node_level,
    )
    solved, flag = call(0, *args)
    cap = lax.axis_size("leaf") - 3
    solved = lax.cond(flag[0, 0] > 0, lambda: call(cap, *args)[0], lambda: solved)
    return jnp.swapaxes(solved, 1, 2)


def solution(mesh):
    in_specs = (
        P("leaf", None, None),
        P("leaf", None, None),
        P("leaf", "blk", None, None, None),
        P("leaf", "blk", None),
        P("leaf", "blk", None),
        P("leaf", "blk"),
        P(),
    )
    out_specs = P("leaf", None, None)
    return jax.shard_map(body, mesh=mesh, in_specs=in_specs, out_specs=out_specs, check_vma=False)
```
